32 devices in a mesh: row: 4 (over z), col: 8 (over y, x, core).
Axes of the slice: x: 2, y: 2, z: 4, core: 2. Of those that a mesh axis runs over, the one named last changes fastest.
Arguments:
- panel: float32 [8, 1024, 8192], P(None, 'row', 'col'), may hold values from -0.0625 to 0.0625
- prior_y: float32 [8192, 1024], P('col', 'row'), may hold values from -6 to 6
- right_side: float32 [8, 1024, 1024], P(None, 'row', 'col'), may hold values from -6 to 6
- inv_blocks: float32 [2, 1024, 1024], P(None, 'row'), may hold values from -2 to 2, as said below
- lower_block: float32 [1024, 1024], P('row'), may hold values from -0.1875 to 0.1875
Outputs:
- y_window: float32 [2, 1024, 1024], P(None, 'row', 'col')
- pending: float32 [6, 1024, 1024], P(None, 'row', 'col')
The draws below stay inside these ranges and needn't reach their ends.
Inputs may be any that keep to these rules, and one draw needn't show every extreme that they name: `inv_blocks`: each block is lower triangular with a positive diagonal.
All inputs are finite; a program needn't handle non-finite values.
Results may differ from the reference program's by a relative error of at most 0.000073.
Values sent between devices are 32-bit elements; how exact they have to be, the bound alone decides.
A program may use at most 64 MiB of HBM per device.

```python
import math
import jax
import jax.numpy as jnp
from jax import lax

BS = 1024
M = 1024
STEPS = 8
PRIOR = 8192


def draw_inv_blocks(key, part):
    key_diag, key_off = jax.random.split(key, 2)
    indices = jnp.arange(BS)
    strict = (indices[:, None] > indices[None, :]).astype(jnp.float32)
    identity = (indices[:, None] == indices[None, :]).astype(jnp.float32)
    diagonal = jnp.exp(jax.random.uniform(key_diag, (2, BS), jnp.float32, math.log(0.5), math.log(2.0)))
    offdiag = jax.random.normal(key_off, (2, BS, BS), jnp.float32) * (0.6 / math.sqrt(BS))
    offdiag = jnp.clip(offdiag, -1.5, 1.5)
    return offdiag * strict + identity * diagonal[:, :, None]


def raised(array, key, source, target, shards_of, factor):
    owner, partner = [(jnp.arange(array.shape[dim]) // (array.shape[dim] // shards_of)).reshape([-1 if axis == dim else 1 for axis in range(array.ndim)]) for dim in (source, target)]
    chosen = jax.random.permutation(key, shards_of)[partner]
    strong = (owner == chosen) | (owner == (partner + shards_of // 2) % shards_of)
    return jnp.where(strong, factor * array, array)


def shard_levels(own_key, extent, cuts, smallest, high):
    gain = 1.0
    for dim, parts in cuts:
        steps = jax.random.uniform(jax.random.fold_in(jax.random.fold_in(own_key, 6), dim), (parts,), jnp.float32, smallest / len(cuts), high / len(cuts))
        gain = gain * jnp.repeat(jnp.exp(steps), extent[dim] // parts).reshape((-1,) + (1,) * (len(extent) - 1 - dim))
    return gain


def gaussian(stream_key, shape, width, reach, shards=(), held_as=jnp.bfloat16):
    entries = width * jax.random.normal(stream_key, shape, jnp.float32)
    if shards:
        entries = entries * shard_levels(stream_key, shape, shards, -0.22, 0.18)
    return jnp.clip(entries, -reach, reach).astype(held_as)


def noise_with(own_key, shape, spread, limit, shards, heavy, held_as=jnp.bfloat16):
    drawn = spread * jax.random.normal(own_key, shape, jnp.float32)
    if shards:
        drawn = drawn * shard_levels(own_key, shape, shards, -0.22, 0.18)
    return jnp.clip(raised(drawn, jax.random.fold_in(own_key, 3), *heavy), -limit, limit).astype(held_as)


def setup_inputs(seed: int = 0) -> dict:
    key_of = jax.random.split(jax.random.key(seed), 6)
    panel = gaussian(key_of[0], (STEPS, BS, PRIOR), PRIOR ** -0.5, 0.0625, ((1, 4), (2, 8)), jnp.float32)
    prior_y = noise_with(key_of[1], (PRIOR, M), 1.0, 6.0, ((0, 8), (1, 4)), (0, 1, 8, 2.0), jnp.float32)
    right_side = gaussian(key_of[2], (STEPS, BS, M), 1.0, 6.0, ((1, 4), (2, 8)), jnp.float32)
    inv_blocks = draw_inv_blocks(jax.random.fold_in(key_of[5], 71), 0)
    lower_block = gaussian(key_of[4], (BS, BS), BS ** -0.5, 0.1875, ((0, 4),), jnp.float32)
    return dict(panel=panel, prior_y=prior_y, right_side=right_side, inv_blocks=inv_blocks, lower_block=lower_block)


def reference(panel, prior_y, right_side, inv_blocks, lower_block):
    highest = lax.Precision.HIGHEST
    panel_total = jnp.einsum("sip,pm->sim", panel, prior_y, precision=highest, preferred_element_type=jnp.float32)
    residual = right_side - panel_total
    first_solution = jnp.dot(inv_blocks[0], residual[0], precision=highest, preferred_element_type=jnp.float32)
    second_residual = residual[1] - jnp.dot(lower_block, first_solution, precision=highest, preferred_element_type=jnp.float32)
    second_solution = jnp.dot(inv_blocks[1], second_residual, precision=highest, preferred_element_type=jnp.float32)
    return (jnp.stack([first_solution, second_solution]), residual[2:])
```

```python
import functools

import jax
import jax.numpy as jnp
from jax import lax
from jax.experimental import pallas as pl
from jax.experimental.pallas import tpu as pltpu
from jax.sharding import PartitionSpec as P

MESH = pl.DeviceIdType.MESH
F32 = jnp.float32
BF16 = jnp.bfloat16


def split(x):
    high = x.astype(BF16)
    return high, (x - high.astype(F32)).astype(BF16)


def kernel(
    panel, prior, right, inv, lower, y_out, pend_out,
    pf, p_hi, p_lo, y_buf, y_cat, core_src, core_dst, part, far_dst, rhs,
    inv0, low2, inv1, inv0_hi, inv0_lo, low2_hi, low2_lo, inv1_hi, inv1_lo,
    r0_all, r1_all, y0_all, s1_all, y1_all, y_land,
    right_sem, own_sem, panel_sem, matrix_sem, y_send, y_recv, core_send, core_recv, far_send, far_recv,
    m_send, m_recv, twin_send, twin_recv, r_send, r_recv, s_send, s_recv, e_send, e_recv,
):
    steps, rows, depth = p_hi.shape
    wide = rhs.shape[2]
    staged = pf.shape[0]
    half, part_rows = depth // 2, rows // 2
    lag = 2
    z = lax.axis_index("row")
    col = lax.axis_index("col")
    y, x, core = col // 4, (col // 2) % 2, col % 2
    chip = col // 2
    sibling = col + 1 - 2 * core
    x_near, y_near = col + 2 - 4 * x, col + 4 - 8 * y
    middle = (z == 1) | (z == 2)
    upper = z // 2
    inner = ((z + 1) // 2) % 2
    line = chip + upper * (3 - 2 * chip)
    z_end, z_other = 3 * upper, 1 + upper + inner * (1 - 2 * upper)

    def block(folded):
        return folded + upper * (3 - 2 * folded)

    def number(digits):
        return sum(d * 8**i for i, d in enumerate(digits))

    line_y, line_x = line // 2, line % 2
    at_end = (1 - line_y) * number((0, 1, 2, 4, 6, 7, 5, 3)) + line_y * (
        (1 - line_x) * number((0, 1, 2, 3, 4, 6, 7, 5)) + line_x * number((0, 1, 2, 3, 4, 6, 5, 7))
    )
    sequence = at_end + inner * (number((2, 3, 0, 4, 1, 6, 7, 5)) - at_end)

    def turn(k):
        digit = (sequence // 8**k) % 8
        return block(digit // 2), digit % 2

    own = [
        pltpu.make_async_copy(prior.at[:, h * wide:(h + 1) * wide], y_buf.at[z, h], own_sem.at[h])
        for h in range(2)
    ]
    for copy in own:
        copy.start()

    def panel_copy(s):
        return pltpu.make_async_copy(panel.at[s], pf.at[s % staged], panel_sem.at[s])

    for s in range(staged):
        panel_copy(s).start()
    right_copy = pltpu.make_async_copy(right, rhs, right_sem)
    right_copy.start()

    barrier = pltpu.get_barrier_semaphore()
    for partner in (sibling, x_near, y_near, x_near + y_near - col):
        pl.semaphore_signal(barrier, inc=1, device_id=(z, partner), device_id_type=MESH)
    for j in range(1, 4):
        pl.semaphore_signal(barrier, inc=1, device_id=((z + j) % 4, col), device_id_type=MESH)
    pl.semaphore_wait(barrier, 7)

    def remote(src, dst, send, recv, target):
        return pltpu.make_async_remote_copy(
            src_ref=src, dst_ref=dst, send_sem=send, recv_sem=recv,
            device_id=target, device_id_type=MESH,
        )

    def y_piece(b, h, p):
        return y_buf.at[b, h, pl.ds(p * half, half)]

    def y_copy(folded, h, p, way, from_prior=False):
        b = block(folded)
        here = y_piece(b, h, p)
        src = prior.at[pl.ds(p * half, half), pl.ds(h * wide, wide)] if from_prior else here
        target = z_other if way else z_end
        return remote(src, here, y_send.at[way, folded, h, p], y_recv.at[b, h, p], (target, col))

    def arrived(b, h, p):
        remote(
            y_piece(b, h, p), y_piece(b, h, p), y_send.at[0, 0, h, p], y_recv.at[b, h, p],
            ((z + 1) % 4, col),
        ).wait_recv()

    def outward(folded, h, p):
        y_copy(folded, h, p, 0, folded == 1).start()

    def inward(folded, h, p):
        y_copy(folded, h, p, 1, folded == 1).start()

    def relay(k):
        def take(folded, h, p):
            arrived(block(folded), h, p)

        if k == 0:
            for p in range(2):
                outward(1, 0, p)
                inward(1, 0, p)
            outward(1, 1, 0)
            pl.when(line > 1)(lambda: outward(1, 1, 1))
        elif k in (1, 2):
            take(0, 0, k - 1)
            inward(0, 0, k - 1)
            take(2, 0, k - 1)
            outward(2, 0, k - 1)
        elif k in (3, 4):
            take(0, 1, k - 3)
            inward(0, 1, k - 3)
            if k == 4:
                inward(1, 1, 0)
                inward(1, 1, 1)
            take(3, 0, k - 3)
            outward(3, 0, k - 3)
        elif k == 5:
            take(3, 1, 0)
            outward(3, 1, 0)
        elif k == 6:
            take(3, 1, 1)
            pl.when(line != 3)(lambda: outward(3, 1, 1))
        else:
            for p in range(2):
                take(2, 1, p)
                outward(2, 1, p)
            pl.when(line == 3)(lambda: outward(3, 1, 1))
            pl.when(line < 2)(lambda: outward(1, 1, 1))

    def core_copy(b, c):
        return remote(
            core_src.at[b, c], core_dst.at[b, c], core_send.at[b, c], core_recv.at[b, c], (z, sibling)
        )

    def detour(b):
        return (1 - inner) * ((block(b) - line + 3) // 6)

    def passes(b):
        return jnp.logical_not(middle) & (line == 1) & (block(b) == 3)

    def far_copy(b, c):
        slot = (x + b) % 2 + 2 * ((y + b // 2) % 2) - 1
        target = 2 * b + core
        return remote(
            part.at[b, c], far_dst.at[slot + detour(b) * (3 - slot), c],
            far_send.at[b, c], far_recv.at[slot + detour(b) * (3 - slot), c],
            (z, target + detour(b) * (x_near - target)),
        )

    def far_arrived(slot, c):
        here = far_dst.at[slot, c]
        remote(here, here, far_send.at[0, c], far_recv.at[slot, c], (z, sibling)).wait_recv()

    def add_core(b, c):
        core_copy(b, c).wait_recv()
        part[b, c] = part[b, c] + core_dst[b, c]

        @pl.when((b != chip) & jnp.logical_not(passes(b)))
        def _():
            far_copy(b, c).start()

    def pass_on(b, low, high):
        @pl.loop(low, high)
        def _(c):
            far_arrived(3, c)
            part[b, c] = part[b, c] + far_dst[3, c]
            far_copy(b, c).start()

    def multiply(k, b, h):
        high, low = split(y_buf[b, h])
        y_cat[:, :wide] = high
        y_cat[:, wide:] = low

        @pl.loop(0, steps)
        def _(c):
            if k == 0:
                panel_copy(c).wait()
                high, low = split(pf[c % staged])
                p_hi[c] = high
                p_lo[c] = low

                @pl.when(c < steps - staged)
                def _():
                    panel_copy(c + staged).start()
            both = jnp.dot(p_hi[c], y_cat[...], preferred_element_type=F32)
            rest = jnp.dot(p_lo[c], y_cat[:, :wide], preferred_element_type=F32)
            terms = both[:, :wide] + (both[:, wide:] + rest)

            @pl.when(core == h)
            def _():
                part[b, c] = terms

                @pl.when(c >= lag)
                def _():
                    add_core(b, c - lag)

            @pl.when(core != h)
            def _():
                core_src[b, c] = terms
                core_copy(b, c).start()

        @pl.when(core == h)
        def _():
            for c in range(steps - lag, steps):
                add_core(b, c)

    matrices = (
        (0, 1, 0), (0, 1, 1), (0, 1, 2), (0, 2, 0), (1, 2, 0),
        (2, 1, 0), (3, 2, 0), (3, 1, 0), (3, 2, 1), (3, 2, 2),
    )

    def matrix_refs(source, kind, half_of):
        width = (source + 1) * rows
        take = pl.ds(half_of * part_rows, part_rows)
        if kind == 0:
            put = pl.ds(pl.multiple_of(source * rows + half_of * part_rows, part_rows), part_rows)
            return inv.at[0, take, :width], inv0.at[put, :width]
        put = pl.ds(pl.multiple_of((source % 2) * rows + half_of * part_rows, part_rows), part_rows)
        if kind == 1:
            return lower.at[take], low2.at[put]
        return inv.at[1, take, :width], inv1.at[put, :width]

    def matrix_copy(i):
        source, target, kind = matrices[i]
        src, dst = matrix_refs(source, kind, core)
        return remote(src, dst, m_send.at[i], m_recv.at[i], (target, col))

    def twin_copy(i):
        source, _, kind = matrices[i]
        here = matrix_refs(source, kind, core)[1]
        return remote(here, here, twin_send.at[i], twin_recv.at[i], (z, sibling))

    def send_matrices(which, finish=False):
        for i, (source, _, _) in enumerate(matrices):
            if i in which:
                @pl.when(z == source)
                def _(i=i):
                    matrix_copy(i).wait_send() if finish else matrix_copy(i).start()

    place = pl.ds(pl.multiple_of((z % 2) * rows, rows), rows)
    mine = pl.ds(pl.multiple_of(z * rows, rows), rows)
    own_matrices = [
        pltpu.make_async_copy(inv.at[0], inv0.at[mine], matrix_sem.at[0]),
        pltpu.make_async_copy(lower, low2.at[place], matrix_sem.at[1]),
        pltpu.make_async_copy(inv.at[1], inv1.at[place], matrix_sem.at[2]),
    ]

    def r0_copy(target, source):
        here = r0_all.at[pl.ds(pl.multiple_of(source * rows, rows), rows)]
        return remote(here, here, r_send.at[target], r_recv.at[source], (target, col))

    def r1_copy():
        here = r1_all.at[place]
        return remote(here, here, r_send.at[0], r_recv.at[4], (z_other, col))

    def r1_arrived():
        other = r1_all.at[pl.ds(pl.multiple_of((1 - z % 2) * rows, rows), rows)]
        remote(other, other, r_send.at[0], r_recv.at[4], (z_end, col)).wait_recv()

    def send_r0(finish=False):
        for target in (2, 1):
            @pl.when(z != target)
            def _(target=target):
                r0_copy(target, z).wait_send() if finish else r0_copy(target, z).start()

    def finish():
        for s in range(steps):
            for slot in range(2):
                far_arrived(slot, s)
            pl.when(middle | (line != 3))(lambda: far_arrived(2, s))
            total = (part[chip, s] + far_dst[0, s]) + (far_dst[1, s] + far_dst[2, s])
            rest = rhs[s] - total
            if s == 0:
                r0_all[mine, :] = rest
                send_r0()
            elif s == 1:
                r1_all[place, :] = rest
                pl.when(jnp.logical_not(middle))(lambda: r1_copy().start())
            else:
                pend_out[s - 2] = rest

    @pl.when(jnp.logical_not(middle) & (line == 3))
    def _():
        far_dst[2] = jnp.zeros((steps, rows, wide), F32)

    @pl.when(middle)
    def _():
        relay(0)

    @pl.when(jnp.logical_not(middle))
    def _():
        for h in range(2):
            for p in range(2):
                y_copy(0, h, p, 1, True).start()

    for k in range(8):
        b, h = turn(k)
        if k == 7:
            right_copy.wait()

            @pl.when(jnp.logical_not(middle) & (core == 0))
            def _():
                finish()

        if k > 0:
            @pl.when(middle)
            def _(k=k):
                relay(k)
        if k < 2:
            own[k].wait()
        else:
            @pl.when(jnp.logical_not(middle))
            def _(b=b, h=h):
                arrived(b, h, 0)
                arrived(b, h, 1)
        multiply(k, b, h)
        passing = passes(b) & (core == h)
        if k > 0:
            pl.when(before[1])(lambda: pass_on(before[0], steps // 2, steps))
        pl.when(passing)(lambda: pass_on(b, 0, steps // 2))
        before = b, passing
        if k == 2:
            send_matrices((0, 1, 2, 6, 8, 9))

            @pl.when(middle)
            def _():
                for copy in own_matrices:
                    copy.start()
        if k == 5:
            send_matrices((3, 7))
        if k == 6:
            send_matrices((4, 5))

    def split_rows(ref, hi, lo, first, width):
        high, low = split(ref[first:first + rows, :width])
        hi[first:first + rows, :width] = high
        lo[first:first + rows, :width] = low

    @pl.when(middle)
    def _():
        for copy in own_matrices:
            copy.wait()
        for target in (1, 2):
            @pl.when(z == target)
            def _(target=target):
                here = [i for i, entry in enumerate(matrices) if entry[1] == target]
                for i in here:
                    matrix_copy(i).wait_recv()
                    twin_copy(i).start()
                for i in here:
                    source, _, kind = matrices[i]
                    other = matrix_refs(source, kind, 1 - core)[1]
                    remote(other, other, twin_send.at[i], twin_recv.at[i], (z, sibling)).wait_recv()
                for k in range(2):
                    split_rows(inv1, inv1_hi, inv1_lo, k * rows, (2 * target - 1 + k) * rows)
        for k in range(4):
            split_rows(inv0, inv0_hi, inv0_lo, k * rows, (k + 1) * rows)
        for k in range(2):
            split_rows(low2, low2_hi, low2_lo, k * rows, 4 * rows)

    @pl.when(middle | (core == 1))
    def _():
        finish()

    def dot3(hi, lo, at, width, value):
        high, low = split(value)
        both = jnp.dot(hi[at, :width], jnp.concatenate([high, low], axis=1), preferred_element_type=F32)
        rest = jnp.dot(lo[at, :width], high, preferred_element_type=F32)
        return both[:, :wide] + (both[:, wide:] + rest)

    def end_copy(i, src):
        return remote(src, y_land.at[i], e_send.at[i], e_recv.at[i], (z_end, col))

    def y_ends():
        at_end = pl.ds(pl.multiple_of(z_end * rows, rows), rows)
        far_place = pl.ds(pl.multiple_of((1 - z % 2) * rows, rows), rows)
        return end_copy(0, y0_all.at[at_end]), end_copy(1, y1_all.at[far_place])

    def s_copy():
        here = s1_all.at[:2 * rows]
        return remote(here, here, s_send, s_recv, (2, col))

    @pl.when(middle)
    def _():
        for source in range(4):
            @pl.when(z != source)
            def _(source=source):
                r0_copy(1, source).wait_recv()
        to_end = y_ends()
        for k in range(4):
            at = slice(k * rows, (k + 1) * rows)
            y0_all[at, :] = dot3(inv0_hi, inv0_lo, at, (k + 1) * rows, r0_all[:(k + 1) * rows, :])
        to_end[0].start()
        r1_arrived()
        two = pl.ds(pl.multiple_of((z - 1) * 2 * rows, 2 * rows), 2 * rows)
        s1_all[two, :] = r1_all[...] - dot3(low2_hi, low2_lo, slice(0, 2 * rows), 4 * rows, y0_all[...])

        @pl.when(z == 1)
        def _():
            s_copy().start()

        @pl.when(z == 2)
        def _():
            s_copy().wait_recv()

        for target in (1, 2):
            @pl.when(z == target)
            def _(target=target):
                for k in range(2):
                    width = (2 * target - 1 + k) * rows
                    at = slice(k * rows, (k + 1) * rows)
                    y1_all[at, :] = dot3(inv1_hi, inv1_lo, at, width, s1_all[:width, :])
        to_end[1].start()
        y_out[0] = y0_all[mine, :]
        y_out[1] = y1_all[place, :]
        for copy in to_end:
            copy.wait_send()

        @pl.when(z == 1)
        def _():
            s_copy().wait_send()

        for target in (1, 2):
            @pl.when(z == target)
            def _(target=target):
                for i, entry in enumerate(matrices):
                    if entry[1] == target:
                        twin_copy(i).wait_send()

    @pl.when(jnp.logical_not(middle))
    def _():
        for i in range(2):
            remote(y_land.at[i], y_land.at[i], e_send.at[i], e_recv.at[i], (z_other, col)).wait_recv()
            y_out[i] = y_land[i]
        r1_copy().wait_send()

    send_r0(True)
    send_matrices(range(len(matrices)), True)

    @pl.when(middle)
    def _():
        for h in range(2):
            for p in range(2):
                for folded in (1, 2, 3):
                    y_copy(folded, h, p, 0, folded == 1).wait_send()
                for folded in (0, 1):
                    y_copy(folded, h, p, 1, folded == 1).wait_send()

    @pl.when(jnp.logical_not(middle))
    def _():
        for h in range(2):
            for p in range(2):
                y_copy(0, h, p, 1, True).wait_send()

    for b in range(4):
        @pl.loop(0, steps)
        def _(c):
            core_copy(b, c).wait_send()

            @pl.when(b != chip)
            def _():
                far_copy(b, c).wait_send()


def fused(panel, prior_y, right_side, inv_blocks, lower_block):
    steps, rows, depth = panel.shape
    own = right_side.shape[2]
    size = inv_blocks.shape[2]
    anywhere = pl.BlockSpec(memory_space=pl.ANY)
    local = pl.BlockSpec(memory_space=pltpu.VMEM)
    dma = pltpu.SemaphoreType.DMA
    return pl.pallas_call(
        kernel,
        out_shape=(
            jax.ShapeDtypeStruct((2, rows, own), F32),
            jax.ShapeDtypeStruct((steps - 2, rows, own), F32),
        ),
        in_specs=[anywhere] * 5,
        out_specs=(local, local),
        scratch_shapes=[
            pltpu.VMEM((4, rows, depth), F32),
            pltpu.VMEM((steps, rows, depth), BF16),
            pltpu.VMEM((steps, rows, depth), BF16),
            pltpu.VMEM((4, 2, depth, own), F32),
            pltpu.VMEM((depth, 2 * own), BF16),
            pltpu.VMEM((4, steps, rows, own), F32),
            pltpu.VMEM((4, steps, rows, own), F32),
            pltpu.VMEM((4, steps, rows, own), F32),
            pltpu.VMEM((4, steps, rows, own), F32),
            pltpu.VMEM((steps, rows, own), F32),
            pltpu.VMEM((size, size), F32),
            pltpu.VMEM((2 * rows, size), F32),
            pltpu.VMEM((2 * rows, size), F32),
            pltpu.VMEM((size, size), BF16),
            pltpu.VMEM((size, size), BF16),
            pltpu.VMEM((2 * rows, size), BF16),
            pltpu.VMEM((2 * rows, size), BF16),
            pltpu.VMEM((2 * rows, size), BF16),
            pltpu.VMEM((2 * rows, size), BF16),
            pltpu.VMEM((size, own), F32),
            pltpu.VMEM((2 * rows, own), F32),
            pltpu.VMEM((size, own), F32),
            pltpu.VMEM((size, own), F32),
            pltpu.VMEM((2 * rows, own), F32),
            pltpu.VMEM((2, rows, own), F32),
            dma,
            dma((2,)),
            dma((steps,)),
            dma((3,)),
            dma((2, 4, 2, 2)),
            dma((4, 2, 2)),
            dma((4, steps)),
            dma((4, steps)),
            dma((4, steps)),
            dma((4, steps)),
            dma((10,)),
            dma((10,)),
            dma((10,)),
            dma((10,)),
            dma((3,)),
            dma((5,)),
            dma,
            dma,
            dma((2,)),
            dma((2,)),
        ],
        compiler_params=pltpu.CompilerParams(
            collective_id=0, has_side_effects=True, vmem_limit_bytes=61 * 1024 * 1024
        ),
    )(panel, prior_y, right_side, inv_blocks, lower_block)


def general(panel, prior_y, right_side, inv_blocks, lower_block):
    highest = lax.Precision.HIGHEST
    terms = jnp.einsum(
        "sip,pm->sim",
        panel,
        lax.all_gather(prior_y, "row", axis=1, tiled=True),
        precision=highest,
        preferred_element_type=jnp.float32,
    )
    panel_total = lax.psum_scatter(terms, "col", scatter_dimension=2, tiled=True)
    residual = right_side - panel_total
    first_all_rows = lax.all_gather(residual[0], "row", axis=0, tiled=True)
    first_solution = jnp.dot(
        inv_blocks[0], first_all_rows, precision=highest, preferred_element_type=jnp.float32
    )
    solved_all = lax.all_gather(first_solution, "row", axis=0, tiled=True)
    second_residual = residual[1] - jnp.dot(
        lower_block, solved_all, precision=highest, preferred_element_type=jnp.float32
    )
    second_all_rows = lax.all_gather(second_residual, "row", axis=0, tiled=True)
    second_solution = jnp.dot(
        inv_blocks[1], second_all_rows, precision=highest, preferred_element_type=jnp.float32
    )
    return (jnp.stack([first_solution, second_solution]), residual[2:])


def solution(mesh):
    placed = (
        P(None, "row", "col"),
        P("col", "row"),
        P(None, "row", "col"),
        P(None, "row", None),
        P("row", None),
    )
    four_by_eight = mesh.shape["row"] == 4 and mesh.shape["col"] == 8
    return jax.shard_map(
        fused if four_by_eight else general,
        mesh=mesh,
        in_specs=placed,
        out_specs=(P(None, "row", "col"), P(None, "row", "col")),
        check_vma=False,
    )
```

```python
import functools

import jax
import jax.numpy as jnp
from jax import lax
from jax.experimental import pallas as pl
from jax.experimental.pallas import tpu as pltpu
from jax.sharding import PartitionSpec as P

MESH = pl.DeviceIdType.MESH
F32 = jnp.float32
BF16 = jnp.bfloat16


def split(x):
    high = x.astype(BF16)
    return high, (x - high.astype(F32)).astype(BF16)


def kernel(
    panel, prior, right, inv, lower, y_out, pend_out,
    pf, p_hi, p_lo, y_buf, y_cat, core_src, core_dst, part, far_dst, rhs,
    inv0, low2, inv1, inv0_hi, inv0_lo, low2_hi, low2_lo, inv1_hi, inv1_lo,
    r0_all, r1_all, y0_all, s1_all, y1_all, y_land,
    right_sem, own_sem, panel_sem, matrix_sem, y_send, y_recv, core_send, core_recv, far_send, far_recv,
    m_send, m_recv, twin_send, twin_recv, r_send, r_recv, s_send, s_recv, e_send, e_recv,
):
    steps, rows, depth = p_hi.shape
    wide = rhs.shape[2]
    staged = pf.shape[0]
    half, part_rows = depth // 2, rows // 2
    lag = 2
    z = lax.axis_index("row")
    col = lax.axis_index("col")
    y, x, core = col // 4, (col // 2) % 2, col % 2
    chip = col // 2
    sibling = col + 1 - 2 * core
    x_near, y_near = col + 2 - 4 * x, col + 4 - 8 * y
    middle = (z == 1) | (z == 2)
    upper = z // 2
    inner = ((z + 1) // 2) % 2
    line = chip + upper * (3 - 2 * chip)
    z_end, z_other = 3 * upper, 1 + upper + inner * (1 - 2 * upper)

    def block(folded):
        return folded + upper * (3 - 2 * folded)

    def number(digits):
        return sum(d * 8**i for i, d in enumerate(digits))

    line_y, line_x = line // 2, line % 2
    at_end = (1 - line_y) * number((0, 1, 2, 4, 6, 7, 5, 3)) + line_y * (
        (1 - line_x) * number((0, 1, 2, 3, 4, 6, 7, 5)) + line_x * number((0, 1, 2, 3, 4, 6, 5, 7))
    )
    sequence = at_end + inner * (number((2, 3, 0, 4, 1, 6, 7, 5)) - at_end)

    def turn(k):
        digit = (sequence // 8**k) % 8
        return block(digit // 2), digit % 2

    own = [
        pltpu.make_async_copy(prior.at[:, h * wide:(h + 1) * wide], y_buf.at[z, h], own_sem.at[h])
        for h in range(2)
    ]
    for copy in own:
        copy.start()

    def panel_copy(s):
        return pltpu.make_async_copy(panel.at[s], pf.at[s % staged], panel_sem.at[s])

    for s in range(staged):
        panel_copy(s).start()
    right_copy = pltpu.make_async_copy(right, rhs, right_sem)
    right_copy.start()

    barrier = pltpu.get_barrier_semaphore()
    for partner in (sibling, x_near, y_near, x_near + y_near - col):
        pl.semaphore_signal(barrier, inc=1, device_id=(z, partner), device_id_type=MESH)
    for j in range(1, 4):
        pl.semaphore_signal(barrier, inc=1, device_id=((z + j) % 4, col), device_id_type=MESH)
    pl.semaphore_wait(barrier, 7)

    def remote(src, dst, send, recv, target):
        return pltpu.make_async_remote_copy(
            src_ref=src, dst_ref=dst, send_sem=send, recv_sem=recv,
            device_id=target, device_id_type=MESH,
        )

    def y_piece(b, h, p):
        return y_buf.at[b, h, pl.ds(p * half, half)]

    def y_copy(folded, h, p, way, from_prior=False):
        b = block(folded)
        here = y_piece(b, h, p)
        src = prior.at[pl.ds(p * half, half), pl.ds(h * wide, wide)] if from_prior else here
        target = z_other if way else z_end
        return remote(src, here, y_send.at[way, folded, h, p], y_recv.at[b, h, p], (target, col))

    def arrived(b, h, p):
        remote(
            y_piece(b, h, p), y_piece(b, h, p), y_send.at[0, 0, h, p], y_recv.at[b, h, p],
            ((z + 1) % 4, col),
        ).wait_recv()

    def outward(folded, h, p):
        y_copy(folded, h, p, 0, folded == 1).start()

    def inward(folded, h, p):
        y_copy(folded, h, p, 1, folded == 1).start()

    def relay(k):
        def take(folded, h, p):
            arrived(block(folded), h, p)

        if k == 0:
            for p in range(2):
                outward(1, 0, p)
                inward(1, 0, p)

            @pl.when(line > 1)
            def _():
                outward(1, 1, 0)
                outward(1, 1, 1)
        elif k in (1, 2):
            take(0, 0, k - 1)
            inward(0, 0, k - 1)
            take(2, 0, k - 1)
            outward(2, 0, k - 1)
        elif k in (3, 4):
            take(0, 1, k - 3)
            inward(0, 1, k - 3)
            if k == 4:
                inward(1, 1, 0)
                inward(1, 1, 1)
            take(3, 0, k - 3)
            outward(3, 0, k - 3)
        elif k == 5:
            take(3, 1, 0)
            pl.when(line != 3)(lambda: outward(3, 1, 0))
        elif k == 6:
            take(3, 1, 1)
            pl.when(line != 3)(lambda: outward(3, 1, 1))
        else:
            for p in range(2):
                take(2, 1, p)
                outward(2, 1, p)
            for p in range(2):
                pl.when(line == 3)(lambda p=p: outward(3, 1, p))
                pl.when(line < 2)(lambda p=p: outward(1, 1, p))

    def core_copy(b, c):
        return remote(
            core_src.at[b, c], core_dst.at[b, c], core_send.at[b, c], core_recv.at[b, c], (z, sibling)
        )

    def detour(b):
        both = block(b) + line
        return (1 - inner) * (1 - line_y) * (both // 3 - both // 4)

    def passes(b):
        return jnp.logical_not(middle) & (block(b) == line + 2)

    def far_copy(b, c):
        slot = (x + b) % 2 + 2 * ((y + b // 2) % 2) - 1
        target = 2 * b + core
        return remote(
            part.at[b, c], far_dst.at[slot + detour(b) * (3 - slot), c],
            far_send.at[b, c], far_recv.at[slot + detour(b) * (3 - slot), c],
            (z, target + detour(b) * (x_near - target)),
        )

    def far_arrived(slot, c):
        here = far_dst.at[slot, c]
        remote(here, here, far_send.at[0, c], far_recv.at[slot, c], (z, sibling)).wait_recv()

    def add_core(b, c):
        core_copy(b, c).wait_recv()
        part[b, c] = part[b, c] + core_dst[b, c]

        @pl.when((b != chip) & jnp.logical_not(passes(b)))
        def _():
            far_copy(b, c).start()

    def pass_on(b, low, high):
        @pl.loop(low, high)
        def _(c):
            far_arrived(3, c)
            part[b, c] = part[b, c] + far_dst[3, c]
            far_copy(b, c).start()

    def multiply(k, b, h):
        high, low = split(y_buf[b, h])
        y_cat[:, :wide] = high
        y_cat[:, wide:] = low

        @pl.loop(0, steps)
        def _(c):
            if k == 0:
                panel_copy(c).wait()
                high, low = split(pf[c % staged])
                p_hi[c] = high
                p_lo[c] = low

                @pl.when(c < steps - staged)
                def _():
                    panel_copy(c + staged).start()
            both = jnp.dot(p_hi[c], y_cat[...], preferred_element_type=F32)
            rest = jnp.dot(p_lo[c], y_cat[:, :wide], preferred_element_type=F32)
            terms = both[:, :wide] + (both[:, wide:] + rest)

            @pl.when(core == h)
            def _():
                part[b, c] = terms

                @pl.when(c >= lag)
                def _():
                    add_core(b, c - lag)

            @pl.when(core != h)
            def _():
                core_src[b, c] = terms
                core_copy(b, c).start()

        @pl.when(core == h)
        def _():
            for c in range(steps - lag, steps):
                add_core(b, c)

    def multiply_last(b, h, before, wait_last):
        groups = ((0, 1), (1, 2), (2, 4), (4, 6), (6, 8))
        for p in range(2):
            here = slice(p * half, (p + 1) * half)
            if p == 1:
                wait_last()
            high, low = split(y_buf[b, h, here])
            y_cat[here, :wide] = high
            y_cat[here, wide:] = low

            def product(c, count):
                left = p_hi[pl.ds(c, count), :, here].reshape(count * rows, half)
                both = jnp.dot(left, y_cat[here, :], preferred_element_type=F32)
                left = p_lo[pl.ds(c, count), :, here].reshape(count * rows, half)
                rest = jnp.dot(left, y_cat[here, :wide], preferred_element_type=F32)
                return (both[:, :wide] + (both[:, wide:] + rest)).reshape(count, rows, wide)

            if p == 0:
                @pl.loop(0, steps // 2)
                def _(i):
                    terms = product(2 * i, 2)

                    @pl.when(core == h)
                    def _():
                        part[b, pl.ds(2 * i, 2)] = terms

                    @pl.when(core != h)
                    def _():
                        core_src[b, pl.ds(2 * i, 2)] = terms
                continue
            for i, (low_c, high_c) in enumerate(groups):
                terms = product(low_c, high_c - low_c)

                @pl.when(core == h)
                def _():
                    part[b, low_c:high_c] = part[b, low_c:high_c] + terms
                    if i > 0:
                        for c in range(*groups[i - 1]):
                            add_core(b, c)

                @pl.when(core != h)
                def _():
                    core_src[b, low_c:high_c] = core_src[b, low_c:high_c] + terms
                    for c in range(low_c, high_c):
                        core_copy(b, c).start()
                if i == 2:
                    @pl.when(jnp.logical_not(middle) & (core == 1) & (line > 1))
                    def _():
                        finish(0, 2)
                    pl.when(before[1])(lambda: pass_on(before[0], 2, 3))
                if i == 3:
                    pl.when(before[1])(lambda: pass_on(before[0], 3, 4))

        @pl.when(core == h)
        def _():
            for c in range(*groups[-1]):
                add_core(b, c)
        pl.when(before[1])(lambda: pass_on(before[0], 4, steps))

    matrices = (
        (0, 1, 0), (0, 1, 1), (0, 1, 2), (0, 2, 0), (1, 2, 0),
        (2, 1, 0), (3, 2, 0), (3, 1, 0), (3, 2, 1), (3, 2, 2),
    )

    def matrix_refs(source, kind, half_of):
        width = (source + 1) * rows
        take = pl.ds(half_of * part_rows, part_rows)
        if kind == 0:
            put = pl.ds(pl.multiple_of(source * rows + half_of * part_rows, part_rows), part_rows)
            return inv.at[0, take, :width], inv0.at[put, :width]
        put = pl.ds(pl.multiple_of((source % 2) * rows + half_of * part_rows, part_rows), part_rows)
        if kind == 1:
            return lower.at[take], low2.at[put]
        return inv.at[1, take, :width], inv1.at[put, :width]

    def matrix_copy(i):
        source, target, kind = matrices[i]
        src, dst = matrix_refs(source, kind, core)
        return remote(src, dst, m_send.at[i], m_recv.at[i], (target, col))

    def twin_copy(i):
        source, _, kind = matrices[i]
        here = matrix_refs(source, kind, core)[1]
        return remote(here, here, twin_send.at[i], twin_recv.at[i], (z, sibling))

    def send_matrices(which, finish=False):
        for i, (source, _, _) in enumerate(matrices):
            if i in which:
                @pl.when(z == source)
                def _(i=i):
                    matrix_copy(i).wait_send() if finish else matrix_copy(i).start()

    place = pl.ds(pl.multiple_of((z % 2) * rows, rows), rows)
    mine = pl.ds(pl.multiple_of(z * rows, rows), rows)
    own_matrices = [
        pltpu.make_async_copy(inv.at[0], inv0.at[mine], matrix_sem.at[0]),
        pltpu.make_async_copy(lower, low2.at[place], matrix_sem.at[1]),
        pltpu.make_async_copy(inv.at[1], inv1.at[place], matrix_sem.at[2]),
    ]

    def r0_copy(target, source):
        here = r0_all.at[pl.ds(pl.multiple_of(source * rows, rows), rows)]
        return remote(here, here, r_send.at[target], r_recv.at[source], (target, col))

    def r1_copy():
        here = r1_all.at[place]
        return remote(here, here, r_send.at[0], r_recv.at[4], (z_other, col))

    def r1_arrived():
        other = r1_all.at[pl.ds(pl.multiple_of((1 - z % 2) * rows, rows), rows)]
        remote(other, other, r_send.at[0], r_recv.at[4], (z_end, col)).wait_recv()

    def send_r0(finish=False):
        for target in (2, 1):
            @pl.when(z != target)
            def _(target=target):
                r0_copy(target, z).wait_send() if finish else r0_copy(target, z).start()

    def finish(low, high):
        for s in range(low, high):
            for slot in range(2):
                far_arrived(slot, s)
            pl.when(middle | (line < 2))(lambda s=s: far_arrived(2, s))
            total = (part[chip, s] + far_dst[0, s]) + (far_dst[1, s] + far_dst[2, s])
            rest = rhs[s] - total
            if s == 0:
                r0_all[mine, :] = rest
                send_r0()
            elif s == 1:
                r1_all[place, :] = rest
                pl.when(jnp.logical_not(middle))(lambda: r1_copy().start())
            else:
                pend_out[s - 2] = rest

    @pl.when(jnp.logical_not(middle) & (line > 1))
    def _():
        far_dst[2] = jnp.zeros((steps, rows, wide), F32)

    @pl.when(middle)
    def _():
        relay(0)

    @pl.when(jnp.logical_not(middle))
    def _():
        for h in range(2):
            for p in range(2):
                y_copy(0, h, p, 1, True).start()

    for k in range(8):
        b, h = turn(k)
        if k == 7:
            right_copy.wait()

            @pl.when(jnp.logical_not(middle) & ((core == 0) | (line == 0)))
            def _():
                finish(0, steps)

        if k > 0:
            @pl.when(middle)
            def _(k=k):
                relay(k)
        if k < 2:
            own[k].wait()
        else:
            @pl.when(jnp.logical_not(middle))
            def _(b=b, h=h, k=k):
                arrived(b, h, 0)
                if k < 7:
                    arrived(b, h, 1)
        if k == 7:
            multiply_last(b, h, before, lambda: pl.when(jnp.logical_not(middle))(lambda: arrived(b, h, 1)))
            continue
        multiply(k, b, h)
        passing = passes(b) & (core == h)
        if k > 0:
            pl.when(before[1])(lambda: pass_on(before[0], steps // 2, steps))
        early = 2 if k == 6 else steps // 2
        pl.when(passing)(lambda: pass_on(b, 0, early))
        before = b, passing
        if k == 2:
            send_matrices((0, 1, 2, 6, 8, 9))

            @pl.when(middle)
            def _():
                for copy in own_matrices:
                    copy.start()
        if k == 5:
            send_matrices((3, 7))
        if k == 6:
            send_matrices((4, 5))

    def split_rows(ref, hi, lo, first, width):
        high, low = split(ref[first:first + rows, :width])
        hi[first:first + rows, :width] = high
        lo[first:first + rows, :width] = low

    @pl.when(middle)
    def _():
        for copy in own_matrices:
            copy.wait()
        for target in (1, 2):
            @pl.when(z == target)
            def _(target=target):
                here = [i for i, entry in enumerate(matrices) if entry[1] == target]
                for i in here:
                    matrix_copy(i).wait_recv()
                    twin_copy(i).start()
                for i in here:
                    source, _, kind = matrices[i]
                    other = matrix_refs(source, kind, 1 - core)[1]
                    remote(other, other, twin_send.at[i], twin_recv.at[i], (z, sibling)).wait_recv()
                for k in range(2):
                    split_rows(inv1, inv1_hi, inv1_lo, k * rows, (2 * target - 1 + k) * rows)
        for k in range(4):
            split_rows(inv0, inv0_hi, inv0_lo, k * rows, (k + 1) * rows)
        for k in range(2):
            split_rows(low2, low2_hi, low2_lo, k * rows, 4 * rows)

    @pl.when(middle | ((core == 1) & (line == 1)))
    def _():
        finish(0, 2)

    @pl.when(jnp.logical_not(middle) & (core == 1) & (line > 0))
    def _():
        finish(2, steps)

    def dot3(hi, lo, at, width, value, first=0):
        high, low = value
        both = jnp.dot(hi[at, first:width], jnp.concatenate([high, low], axis=1), preferred_element_type=F32)
        rest = jnp.dot(lo[at, first:width], high, preferred_element_type=F32)
        return both[:, :wide] + (both[:, wide:] + rest)

    def end_copy(i, src):
        return remote(src, y_land.at[i], e_send.at[i], e_recv.at[i], (z_end, col))

    def y_ends():
        at_end = pl.ds(pl.multiple_of(z_end * rows, rows), rows)
        far_place = pl.ds(pl.multiple_of((1 - z % 2) * rows, rows), rows)
        return end_copy(0, y0_all.at[at_end]), end_copy(1, y1_all.at[far_place])

    def s_copy(k):
        here = s1_all.at[k * rows:(k + 1) * rows]
        return remote(here, here, s_send.at[k], s_recv.at[k], (2, col))

    @pl.when(middle)
    def _():
        to_end = y_ends()

        def r0_split(source):
            @pl.when(z != source)
            def _():
                r0_copy(1, source).wait_recv()
            return split(r0_all[source * rows:(source + 1) * rows, :])

        def columns(ref_hi, ref_lo, first, source, value):
            high, low = value
            here = slice(source * rows, (source + 1) * rows)
            both = jnp.dot(ref_hi[first:, here], jnp.concatenate([high, low], axis=1), preferred_element_type=F32)
            rest = jnp.dot(ref_lo[first:, here], high, preferred_element_type=F32)
            return both[:, :wide] + (both[:, wide:] + rest)

        for source in (1, 2, 0, 3):
            first = source * rows
            terms = columns(inv0_hi, inv0_lo, first, source, r0_split(source))
            if source == 1:
                y0_all[:rows, :] = jnp.zeros((rows, wide), F32)
                y0_all[rows:, :] = terms
            else:
                y0_all[first:, :] = y0_all[first:, :] + terms
        to_end[0].start()
        r1_arrived()
        solved = split(y0_all[...])

        def second(k):
            at = slice(k * rows, (k + 1) * rows)
            return r1_all[at, :] - dot3(low2_hi, low2_lo, at, 4 * rows, solved)

        def s1_rows(k):
            return s1_all[:k * rows, :]

        @pl.when(z == 1)
        def _():
            for k in range(2):
                s1_all[k * rows:(k + 1) * rows, :] = second(k)
                s_copy(k).start()
            for k in range(2):
                at = slice(k * rows, (k + 1) * rows)
                y1_all[at, :] = dot3(inv1_hi, inv1_lo, at, (k + 1) * rows, split(s1_rows(k + 1)))
                if k == 0:
                    to_end[1].start()

        @pl.when(z == 2)
        def _():
            for k in range(2):
                s1_all[(2 + k) * rows:(3 + k) * rows, :] = second(k)
            own_s1 = split(s1_all[2 * rows:, :])
            for k in range(2):
                at = slice(k * rows, (k + 1) * rows)
                value = tuple(v[:(k + 1) * rows] for v in own_s1)
                y1_all[at, :] = dot3(inv1_hi, inv1_lo, at, (3 + k) * rows, value, 2 * rows)
            for k in range(2):
                s_copy(k).wait_recv()
            far_s1 = split(s1_rows(2))
            for k in (1, 0):
                at = slice(k * rows, (k + 1) * rows)
                y1_all[at, :] = y1_all[at, :] + dot3(inv1_hi, inv1_lo, at, 2 * rows, far_s1)
                if k == 1:
                    to_end[1].start()

        finish(2, steps)
        y_out[0] = y0_all[mine, :]
        y_out[1] = y1_all[place, :]
        for copy in to_end:
            copy.wait_send()

        @pl.when(z == 1)
        def _():
            for k in range(2):
                s_copy(k).wait_send()

        for target in (1, 2):
            @pl.when(z == target)
            def _(target=target):
                for i, entry in enumerate(matrices):
                    if entry[1] == target:
                        twin_copy(i).wait_send()

    @pl.when(jnp.logical_not(middle))
    def _():
        for i in range(2):
            remote(y_land.at[i], y_land.at[i], e_send.at[i], e_recv.at[i], (z_other, col)).wait_recv()
            y_out[i] = y_land[i]
        r1_copy().wait_send()

    send_r0(True)
    send_matrices(range(len(matrices)), True)

    @pl.when(middle)
    def _():
        for h in range(2):
            for p in range(2):
                for folded in (1, 2, 3):
                    y_copy(folded, h, p, 0, folded == 1).wait_send()
                for folded in (0, 1):
                    y_copy(folded, h, p, 1, folded == 1).wait_send()

    @pl.when(jnp.logical_not(middle))
    def _():
        for h in range(2):
            for p in range(2):
                y_copy(0, h, p, 1, True).wait_send()

    for b in range(4):
        @pl.loop(0, steps)
        def _(c):
            core_copy(b, c).wait_send()

            @pl.when(b != chip)
            def _():
                far_copy(b, c).wait_send()


def fused(panel, prior_y, right_side, inv_blocks, lower_block):
    steps, rows, depth = panel.shape
    own = right_side.shape[2]
    size = inv_blocks.shape[2]
    anywhere = pl.BlockSpec(memory_space=pl.ANY)
    local = pl.BlockSpec(memory_space=pltpu.VMEM)
    dma = pltpu.SemaphoreType.DMA
    return pl.pallas_call(
        kernel,
        out_shape=(
            pltpu.VMEM((2, rows, own), F32),
            pltpu.VMEM((steps - 2, rows, own), F32),
        ),
        in_specs=[anywhere] * 5,
        out_specs=(local, local),
        scratch_shapes=[
            pltpu.VMEM((4, rows, depth), F32),
            pltpu.VMEM((steps, rows, depth), BF16),
            pltpu.VMEM((steps, rows, depth), BF16),
            pltpu.VMEM((4, 2, depth, own), F32),
            pltpu.VMEM((depth, 2 * own), BF16),
            pltpu.VMEM((4, steps, rows, own), F32),
            pltpu.VMEM((4, steps, rows, own), F32),
            pltpu.VMEM((4, steps, rows, own), F32),
            pltpu.VMEM((4, steps, rows, own), F32),
            pltpu.VMEM((steps, rows, own), F32),
            pltpu.VMEM((size, size), F32),
            pltpu.VMEM((2 * rows, size), F32),
            pltpu.VMEM((2 * rows, size), F32),
            pltpu.VMEM((size, size), BF16),
            pltpu.VMEM((size, size), BF16),
            pltpu.VMEM((2 * rows, size), BF16),
            pltpu.VMEM((2 * rows, size), BF16),
            pltpu.VMEM((2 * rows, size), BF16),
            pltpu.VMEM((2 * rows, size), BF16),
            pltpu.VMEM((size, own), F32),
            pltpu.VMEM((2 * rows, own), F32),
            pltpu.VMEM((size, own), F32),
            pltpu.VMEM((size, own), F32),
            pltpu.VMEM((2 * rows, own), F32),
            pltpu.VMEM((2, rows, own), F32),
            dma,
            dma((2,)),
            dma((steps,)),
            dma((3,)),
            dma((2, 4, 2, 2)),
            dma((4, 2, 2)),
            dma((4, steps)),
            dma((4, steps)),
            dma((4, steps)),
            dma((4, steps)),
            dma((10,)),
            dma((10,)),
            dma((10,)),
            dma((10,)),
            dma((3,)),
            dma((5,)),
            dma((2,)),
            dma((2,)),
            dma((2,)),
            dma((2,)),
        ],
        compiler_params=pltpu.CompilerParams(
            collective_id=0, has_side_effects=True, vmem_limit_bytes=61 * 1024 * 1024
        ),
    )(panel, prior_y, right_side, inv_blocks, lower_block)


def general(panel, prior_y, right_side, inv_blocks, lower_block):
    highest = lax.Precision.HIGHEST
    terms = jnp.einsum(
        "sip,pm->sim",
        panel,
        lax.all_gather(prior_y, "row", axis=1, tiled=True),
        precision=highest,
        preferred_element_type=jnp.float32,
    )
    panel_total = lax.psum_scatter(terms, "col", scatter_dimension=2, tiled=True)
    residual = right_side - panel_total
    first_all_rows = lax.all_gather(residual[0], "row", axis=0, tiled=True)
    first_solution = jnp.dot(
        inv_blocks[0], first_all_rows, precision=highest, preferred_element_type=jnp.float32
    )
    solved_all = lax.all_gather(first_solution, "row", axis=0, tiled=True)
    second_residual = residual[1] - jnp.dot(
        lower_block, solved_all, precision=highest, preferred_element_type=jnp.float32
    )
    second_all_rows = lax.all_gather(second_residual, "row", axis=0, tiled=True)
    second_solution = jnp.dot(
        inv_blocks[1], second_all_rows, precision=highest, preferred_element_type=jnp.float32
    )
    return (jnp.stack([first_solution, second_solution]), residual[2:])


def solution(mesh):
    placed = (
        P(None, "row", "col"),
        P("col", "row"),
        P(None, "row", "col"),
        P(None, "row", None),
        P("row", None),
    )
    four_by_eight = mesh.shape["row"] == 4 and mesh.shape["col"] == 8
    return jax.shard_map(
        fused if four_by_eight else general,
        mesh=mesh,
        in_specs=placed,
        out_specs=(P(None, "row", "col"), P(None, "row", "col")),
        check_vma=False,
    )
```

```python
import functools

import jax
import jax.numpy as jnp
from jax import lax
from jax.experimental import pallas as pl
from jax.experimental.pallas import tpu as pltpu
from jax.sharding import PartitionSpec as P

MESH = pl.DeviceIdType.MESH
F32 = jnp.float32
BF16 = jnp.bfloat16


def split(x):
    high = x.astype(BF16)
    return high, (x - high.astype(F32)).astype(BF16)


def kernel(
    panel, prior, right, inv, lower, y_out, pend_out,
    pf, p_hi, p_lo, y_buf, y_cat, core_src, core_dst, part, far_dst, rhs,
    inv0, low2, inv1, inv0_hi, inv0_lo, low2_hi, low2_lo, inv1_hi, inv1_lo,
    r0_all, r1_all, y0_all, s1_all, y1_all, y_land,
    right_sem, own_sem, panel_sem, matrix_sem, y_send, y_recv, core_send, core_recv, far_send, far_recv,
    m_send, m_recv, twin_send, twin_recv, r_send, r_recv, s_send, s_recv, e_send, e_recv,
):
    steps, rows, depth = p_hi.shape
    wide = rhs.shape[2]
    staged = pf.shape[0]
    half, part_rows = depth // 2, rows // 2
    lag = 2
    z = lax.axis_index("row")
    col = lax.axis_index("col")
    y, x, core = col // 4, (col // 2) % 2, col % 2
    chip = col // 2
    sibling = col + 1 - 2 * core
    x_near, y_near = col + 2 - 4 * x, col + 4 - 8 * y
    middle = (z == 1) | (z == 2)
    upper = z // 2
    inner = ((z + 1) // 2) % 2
    line = chip + upper * (3 - 2 * chip)
    z_end, z_other = 3 * upper, 1 + upper + inner * (1 - 2 * upper)

    def block(folded):
        return folded + upper * (3 - 2 * folded)

    def number(digits):
        return sum(d * 8**i for i, d in enumerate(digits))

    line_y, line_x = line // 2, line % 2
    at_end = (1 - line_y) * number((0, 1, 2, 4, 6, 7, 5, 3)) + line_y * (
        (1 - line_x) * number((0, 1, 2, 3, 4, 6, 7, 5)) + line_x * number((0, 1, 2, 3, 4, 6, 5, 7))
    )
    sequence = at_end + inner * (number((2, 3, 0, 4, 1, 6, 7, 5)) - at_end)

    def turn(k):
        digit = (sequence // 8**k) % 8
        return block(digit // 2), digit % 2

    barrier = pltpu.get_barrier_semaphore()
    for partner in (sibling, x_near, y_near, x_near + y_near - col):
        pl.semaphore_signal(barrier, inc=1, device_id=(z, partner), device_id_type=MESH)
    for j in range(1, 4):
        pl.semaphore_signal(barrier, inc=1, device_id=((z + j) % 4, col), device_id_type=MESH)
    own = [
        pltpu.make_async_copy(prior.at[:, h * wide:(h + 1) * wide], y_buf.at[z, h], own_sem.at[h])
        for h in range(2)
    ]
    for copy in own:
        copy.start()

    def panel_copy(s):
        return pltpu.make_async_copy(panel.at[s], pf.at[s % staged], panel_sem.at[s])

    for s in range(staged):
        panel_copy(s).start()
    right_copy = pltpu.make_async_copy(right, rhs, right_sem)
    right_copy.start()

    pl.semaphore_wait(barrier, 7)

    def remote(src, dst, send, recv, target):
        return pltpu.make_async_remote_copy(
            src_ref=src, dst_ref=dst, send_sem=send, recv_sem=recv,
            device_id=target, device_id_type=MESH,
        )

    def y_piece(b, h, p):
        return y_buf.at[b, h, pl.ds(p * half, half)]

    def y_copy(folded, h, p, way, from_prior=False):
        b = block(folded)
        here = y_piece(b, h, p)
        src = prior.at[pl.ds(p * half, half), pl.ds(h * wide, wide)] if from_prior else here
        target = z_other if way else z_end
        return remote(src, here, y_send.at[way, folded, h, p], y_recv.at[b, h, p], (target, col))

    def arrived(b, h, p):
        remote(
            y_piece(b, h, p), y_piece(b, h, p), y_send.at[0, 0, h, p], y_recv.at[b, h, p],
            ((z + 1) % 4, col),
        ).wait_recv()

    def outward(folded, h, p):
        y_copy(folded, h, p, 0, folded == 1).start()

    def inward(folded, h, p):
        y_copy(folded, h, p, 1, folded == 1).start()

    def relay(k):
        def take(folded, h, p):
            arrived(block(folded), h, p)

        if k == 0:
            for p in range(2):
                outward(1, 0, p)
                inward(1, 0, p)

            @pl.when(line > 1)
            def _():
                outward(1, 1, 0)
                outward(1, 1, 1)
        elif k in (1, 2):
            take(0, 0, k - 1)
            inward(0, 0, k - 1)
            take(2, 0, k - 1)
            outward(2, 0, k - 1)
        elif k in (3, 4):
            take(0, 1, k - 3)
            inward(0, 1, k - 3)
            if k == 4:
                inward(1, 1, 0)
                inward(1, 1, 1)
            take(3, 0, k - 3)
            outward(3, 0, k - 3)
        elif k == 5:
            take(3, 1, 0)
            pl.when(line != 3)(lambda: outward(3, 1, 0))
        elif k == 6:
            take(3, 1, 1)
            pl.when(line != 3)(lambda: outward(3, 1, 1))
        else:
            for p in range(2):
                take(2, 1, p)
                outward(2, 1, p)
            for p in range(2):
                pl.when(line == 3)(lambda p=p: outward(3, 1, p))
                pl.when(line < 2)(lambda p=p: outward(1, 1, p))

    def core_copy(b, c):
        return remote(
            core_src.at[b, c], core_dst.at[b, c], core_send.at[b, c], core_recv.at[b, c], (z, sibling)
        )

    def detour(b):
        both = block(b) + line
        return (1 - inner) * (1 - line_y) * (both // 3 - both // 4)

    def passes(b):
        return jnp.logical_not(middle) & (block(b) == line + 2)

    def far_copy(b, c):
        slot = (x + b) % 2 + 2 * ((y + b // 2) % 2) - 1
        target = 2 * b + core
        return remote(
            part.at[b, c], far_dst.at[slot + detour(b) * (3 - slot), c],
            far_send.at[b, c], far_recv.at[slot + detour(b) * (3 - slot), c],
            (z, target + detour(b) * (x_near - target)),
        )

    def far_arrived(slot, c):
        here = far_dst.at[slot, c]
        remote(here, here, far_send.at[0, c], far_recv.at[slot, c], (z, sibling)).wait_recv()

    def add_core(b, c):
        core_copy(b, c).wait_recv()
        part[b, c] = part[b, c] + core_dst[b, c]

        @pl.when((b != chip) & jnp.logical_not(passes(b)))
        def _():
            far_copy(b, c).start()

    def pass_on(b, low, high):
        @pl.loop(low, high)
        def _(c):
            far_arrived(3, c)
            part[b, c] = part[b, c] + far_dst[3, c]
            far_copy(b, c).start()

    def multiply(k, b, h):
        high, low = split(y_buf[b, h])
        y_cat[:, :wide] = high
        y_cat[:, wide:] = low

        @pl.loop(0, steps)
        def _(c):
            if k == 0:
                panel_copy(c).wait()
                high, low = split(pf[c % staged])
                p_hi[c] = high
                p_lo[c] = low

                @pl.when(c < steps - staged)
                def _():
                    panel_copy(c + staged).start()
            both = jnp.dot(p_hi[c], y_cat[...], preferred_element_type=F32)
            rest = jnp.dot(p_lo[c], y_cat[:, :wide], preferred_element_type=F32)
            terms = both[:, :wide] + (both[:, wide:] + rest)

            @pl.when(core == h)
            def _():
                part[b, c] = terms

                @pl.when(c >= lag)
                def _():
                    add_core(b, c - lag)

            @pl.when(core != h)
            def _():
                core_src[b, c] = terms
                core_copy(b, c).start()

        @pl.when(core == h)
        def _():
            for c in range(steps - lag, steps):
                add_core(b, c)

    def multiply_last(b, h, before, wait_last):
        groups = ((0, 1), (1, 2), (2, 4), (4, 6), (6, 8))
        for p in range(2):
            here = slice(p * half, (p + 1) * half)
            if p == 1:
                wait_last()
            high, low = split(y_buf[b, h, here])
            y_cat[here, :wide] = high
            y_cat[here, wide:] = low

            def product(c, count):
                left = p_hi[pl.ds(c, count), :, here].reshape(count * rows, half)
                both = jnp.dot(left, y_cat[here, :], preferred_element_type=F32)
                left = p_lo[pl.ds(c, count), :, here].reshape(count * rows, half)
                rest = jnp.dot(left, y_cat[here, :wide], preferred_element_type=F32)
                return (both[:, :wide] + (both[:, wide:] + rest)).reshape(count, rows, wide)

            if p == 0:
                @pl.loop(0, steps // 2)
                def _(i):
                    terms = product(2 * i, 2)

                    @pl.when(core == h)
                    def _():
                        part[b, pl.ds(2 * i, 2)] = terms

                    @pl.when(core != h)
                    def _():
                        core_src[b, pl.ds(2 * i, 2)] = terms
                continue
            for i, (low_c, high_c) in enumerate(groups):
                terms = product(low_c, high_c - low_c)

                @pl.when(core == h)
                def _():
                    part[b, low_c:high_c] = part[b, low_c:high_c] + terms
                    if i > 0:
                        for c in range(*groups[i - 1]):
                            add_core(b, c)

                @pl.when(core != h)
                def _():
                    core_src[b, low_c:high_c] = core_src[b, low_c:high_c] + terms
                    for c in range(low_c, high_c):
                        core_copy(b, c).start()
                if i == 2:
                    @pl.when(jnp.logical_not(middle) & (core == 1) & (line > 1))
                    def _():
                        finish(0, 2)
                    pl.when(before[1])(lambda: pass_on(before[0], 2, 3))
                if i == 3:
                    pl.when(before[1])(lambda: pass_on(before[0], 3, 4))

        @pl.when(core == h)
        def _():
            for c in range(*groups[-1]):
                add_core(b, c)
        pl.when(before[1])(lambda: pass_on(before[0], 4, steps))

    matrices = (
        (0, 1, 0), (0, 1, 1), (0, 1, 2), (0, 2, 0), (1, 2, 0),
        (2, 1, 0), (3, 2, 0), (3, 1, 0), (3, 2, 1), (3, 2, 2),
    )

    def matrix_refs(source, kind, half_of):
        width = (source + 1) * rows
        take = pl.ds(half_of * part_rows, part_rows)
        if kind == 0:
            put = pl.ds(pl.multiple_of(source * rows + half_of * part_rows, part_rows), part_rows)
            return inv.at[0, take, :width], inv0.at[put, :width]
        put = pl.ds(pl.multiple_of((source % 2) * rows + half_of * part_rows, part_rows), part_rows)
        if kind == 1:
            return lower.at[take], low2.at[put]
        return inv.at[1, take, :width], inv1.at[put, :width]

    def matrix_copy(i):
        source, target, kind = matrices[i]
        src, dst = matrix_refs(source, kind, core)
        return remote(src, dst, m_send.at[i], m_recv.at[i], (target, col))

    def twin_copy(i):
        source, _, kind = matrices[i]
        here = matrix_refs(source, kind, core)[1]
        return remote(here, here, twin_send.at[i], twin_recv.at[i], (z, sibling))

    def send_matrices(which, finish=False):
        for i, (source, _, _) in enumerate(matrices):
            if i in which:
                @pl.when(z == source)
                def _(i=i):
                    matrix_copy(i).wait_send() if finish else matrix_copy(i).start()

    place = pl.ds(pl.multiple_of((z % 2) * rows, rows), rows)
    mine = pl.ds(pl.multiple_of(z * rows, rows), rows)
    own_matrices = [
        pltpu.make_async_copy(inv.at[0], inv0.at[mine], matrix_sem.at[0]),
        pltpu.make_async_copy(lower, low2.at[place], matrix_sem.at[1]),
        pltpu.make_async_copy(inv.at[1], inv1.at[place], matrix_sem.at[2]),
    ]

    def r0_copy(target, source):
        here = r0_all.at[pl.ds(pl.multiple_of(source * rows, rows), rows)]
        return remote(here, here, r_send.at[target], r_recv.at[source], (target, col))

    def r1_copy():
        here = r1_all.at[place]
        return remote(here, here, r_send.at[0], r_recv.at[4], (z_other, col))

    def r1_arrived():
        other = r1_all.at[pl.ds(pl.multiple_of((1 - z % 2) * rows, rows), rows)]
        remote(other, other, r_send.at[0], r_recv.at[4], (z_end, col)).wait_recv()

    def send_r0(finish=False):
        for target in (2, 1):
            @pl.when(z != target)
            def _(target=target):
                r0_copy(target, z).wait_send() if finish else r0_copy(target, z).start()

    def finish(low, high):
        for s in range(low, high):
            for slot in range(2):
                far_arrived(slot, s)
            pl.when(middle | (line < 2))(lambda s=s: far_arrived(2, s))
            total = (part[chip, s] + far_dst[0, s]) + (far_dst[1, s] + far_dst[2, s])
            rest = rhs[s] - total
            if s == 0:
                r0_all[mine, :] = rest
                send_r0()
            elif s == 1:
                r1_all[place, :] = rest
                pl.when(jnp.logical_not(middle))(lambda: r1_copy().start())
            else:
                pend_out[s - 2] = rest

    @pl.when(jnp.logical_not(middle) & (line > 1))
    def _():
        far_dst[2] = jnp.zeros((steps, rows, wide), F32)

    @pl.when(middle)
    def _():
        relay(0)

    @pl.when(jnp.logical_not(middle))
    def _():
        for h in range(2):
            for p in range(2):
                y_copy(0, h, p, 1, True).start()

    for k in range(8):
        b, h = turn(k)
        if k == 6:
            right_copy.wait()

            @pl.when(jnp.logical_not(middle) & ((core == 0) | (line == 0)))
            def _():
                finish(0, 2)
        if k == 7:
            @pl.when(jnp.logical_not(middle) & ((core == 0) | (line == 0)))
            def _():
                finish(2, steps)

        if k > 0:
            @pl.when(middle)
            def _(k=k):
                relay(k)
        if k < 2:
            own[k].wait()
        else:
            @pl.when(jnp.logical_not(middle))
            def _(b=b, h=h, k=k):
                arrived(b, h, 0)
                if k < 7:
                    arrived(b, h, 1)
        if k == 7:
            multiply_last(b, h, before, lambda: pl.when(jnp.logical_not(middle))(lambda: arrived(b, h, 1)))
            continue
        multiply(k, b, h)
        passing = passes(b) & (core == h)
        if k > 0:
            pl.when(before[1])(lambda: pass_on(before[0], steps // 2, steps))
        early = 2 if k == 6 else steps // 2
        pl.when(passing)(lambda: pass_on(b, 0, early))
        before = b, passing
        if k == 2:
            send_matrices((0, 1, 2, 6, 8, 9))

            @pl.when(middle)
            def _():
                for copy in own_matrices:
                    copy.start()
        if k == 5:
            send_matrices((3, 7))
        if k == 6:
            send_matrices((4, 5))

    def split_rows(ref, hi, lo, first, width):
        high, low = split(ref[first:first + rows, :width])
        hi[first:first + rows, :width] = high
        lo[first:first + rows, :width] = low

    @pl.when(middle)
    def _():
        for copy in own_matrices:
            copy.wait()
        for target in (1, 2):
            @pl.when(z == target)
            def _(target=target):
                here = [i for i, entry in enumerate(matrices) if entry[1] == target]
                for i in here:
                    matrix_copy(i).wait_recv()
                    twin_copy(i).start()
                for i in here:
                    source, _, kind = matrices[i]
                    other = matrix_refs(source, kind, 1 - core)[1]
                    remote(other, other, twin_send.at[i], twin_recv.at[i], (z, sibling)).wait_recv()
                for k in range(2):
                    split_rows(inv1, inv1_hi, inv1_lo, k * rows, (2 * target - 1 + k) * rows)
        for k in range(4):
            split_rows(inv0, inv0_hi, inv0_lo, k * rows, (k + 1) * rows)
        for k in range(2):
            split_rows(low2, low2_hi, low2_lo, k * rows, 4 * rows)

    @pl.when(middle | ((core == 1) & (line == 1)))
    def _():
        finish(0, 2)

    @pl.when(jnp.logical_not(middle) & (core == 1) & (line > 0))
    def _():
        finish(2, steps)

    def dot3(hi, lo, at, width, value, first=0):
        high, low = value
        both = jnp.dot(hi[at, first:width], jnp.concatenate([high, low], axis=1), preferred_element_type=F32)
        rest = jnp.dot(lo[at, first:width], high, preferred_element_type=F32)
        return both[:, :wide] + (both[:, wide:] + rest)

    def end_copy(i, src):
        return remote(src, y_land.at[i], e_send.at[i], e_recv.at[i], (z_end, col))

    def y_ends():
        at_end = pl.ds(pl.multiple_of(z_end * rows, rows), rows)
        far_place = pl.ds(pl.multiple_of((1 - z % 2) * rows, rows), rows)
        return end_copy(0, y0_all.at[at_end]), end_copy(1, y1_all.at[far_place])

    def s_copy(k):
        here = s1_all.at[k * rows:(k + 1) * rows]
        return remote(here, here, s_send.at[k], s_recv.at[k], (2, col))

    @pl.when(middle)
    def _():
        to_end = y_ends()

        def r0_split(source):
            @pl.when(z != source)
            def _():
                r0_copy(1, source).wait_recv()
            return split(r0_all[source * rows:(source + 1) * rows, :])

        def columns(ref_hi, ref_lo, first, source, value):
            high, low = value
            here = slice(source * rows, (source + 1) * rows)
            both = jnp.dot(ref_hi[first:, here], jnp.concatenate([high, low], axis=1), preferred_element_type=F32)
            rest = jnp.dot(ref_lo[first:, here], high, preferred_element_type=F32)
            return both[:, :wide] + (both[:, wide:] + rest)

        for source in (1, 2, 0, 3):
            first = source * rows
            terms = columns(inv0_hi, inv0_lo, first, source, r0_split(source))
            if source == 1:
                y0_all[:rows, :] = jnp.zeros((rows, wide), F32)
                y0_all[rows:, :] = terms
            else:
                y0_all[first:, :] = y0_all[first:, :] + terms
        to_end[0].start()
        r1_arrived()
        solved = split(y0_all[...])

        def second(k):
            at = slice(k * rows, (k + 1) * rows)
            return r1_all[at, :] - dot3(low2_hi, low2_lo, at, 4 * rows, solved)

        def s1_rows(k):
            return s1_all[:k * rows, :]

        @pl.when(z == 1)
        def _():
            for k in range(2):
                s1_all[k * rows:(k + 1) * rows, :] = second(k)
                s_copy(k).start()
            for k in range(2):
                at = slice(k * rows, (k + 1) * rows)
                y1_all[at, :] = dot3(inv1_hi, inv1_lo, at, (k + 1) * rows, split(s1_rows(k + 1)))
                if k == 0:
                    to_end[1].start()

        @pl.when(z == 2)
        def _():
            for k in range(2):
                s1_all[(2 + k) * rows:(3 + k) * rows, :] = second(k)
            own_s1 = split(s1_all[2 * rows:, :])
            for k in range(2):
                at = slice(k * rows, (k + 1) * rows)
                value = tuple(v[:(k + 1) * rows] for v in own_s1)
                y1_all[at, :] = dot3(inv1_hi, inv1_lo, at, (3 + k) * rows, value, 2 * rows)
            for k in range(2):
                s_copy(k).wait_recv()
            far_s1 = split(s1_rows(2))
            for k in (1, 0):
                at = slice(k * rows, (k + 1) * rows)
                y1_all[at, :] = y1_all[at, :] + dot3(inv1_hi, inv1_lo, at, 2 * rows, far_s1)
                if k == 1:
                    to_end[1].start()

        finish(2, steps)
        y_out[0] = y0_all[mine, :]
        y_out[1] = y1_all[place, :]
        for copy in to_end:
            copy.wait_send()

        @pl.when(z == 1)
        def _():
            for k in range(2):
                s_copy(k).wait_send()

        for target in (1, 2):
            @pl.when(z == target)
            def _(target=target):
                for i, entry in enumerate(matrices):
                    if entry[1] == target:
                        twin_copy(i).wait_send()

    @pl.when(jnp.logical_not(middle))
    def _():
        for i in range(2):
            remote(y_land.at[i], y_land.at[i], e_send.at[i], e_recv.at[i], (z_other, col)).wait_recv()
            y_out[i] = y_land[i]
        r1_copy().wait_send()

    send_r0(True)
    send_matrices(range(len(matrices)), True)

    @pl.when(middle)
    def _():
        for h in range(2):
            for p in range(2):
                for folded in (1, 2, 3):
                    y_copy(folded, h, p, 0, folded == 1).wait_send()
                for folded in (0, 1):
                    y_copy(folded, h, p, 1, folded == 1).wait_send()

    @pl.when(jnp.logical_not(middle))
    def _():
        for h in range(2):
            for p in range(2):
                y_copy(0, h, p, 1, True).wait_send()

    for b in range(4):
        @pl.loop(0, steps)
        def _(c):
            core_copy(b, c).wait_send()

            @pl.when(b != chip)
            def _():
                far_copy(b, c).wait_send()


def fused(panel, prior_y, right_side, inv_blocks, lower_block):
    steps, rows, depth = panel.shape
    own = right_side.shape[2]
    size = inv_blocks.shape[2]
    anywhere = pl.BlockSpec(memory_space=pl.ANY)
    local = pl.BlockSpec(memory_space=pltpu.VMEM)
    dma = pltpu.SemaphoreType.DMA
    return pl.pallas_call(
        kernel,
        out_shape=(
            pltpu.VMEM((2, rows, own), F32),
            pltpu.VMEM((steps - 2, rows, own), F32),
        ),
        in_specs=[anywhere] * 5,
        out_specs=(local, local),
        scratch_shapes=[
            pltpu.VMEM((4, rows, depth), F32),
            pltpu.VMEM((steps, rows, depth), BF16),
            pltpu.VMEM((steps, rows, depth), BF16),
            pltpu.VMEM((4, 2, depth, own), F32),
            pltpu.VMEM((depth, 2 * own), BF16),
            pltpu.VMEM((4, steps, rows, own), F32),
            pltpu.VMEM((4, steps, rows, own), F32),
            pltpu.VMEM((4, steps, rows, own), F32),
            pltpu.VMEM((4, steps, rows, own), F32),
            pltpu.VMEM((steps, rows, own), F32),
            pltpu.VMEM((size, size), F32),
            pltpu.VMEM((2 * rows, size), F32),
            pltpu.VMEM((2 * rows, size), F32),
            pltpu.VMEM((size, size), BF16),
            pltpu.VMEM((size, size), BF16),
            pltpu.VMEM((2 * rows, size), BF16),
            pltpu.VMEM((2 * rows, size), BF16),
            pltpu.VMEM((2 * rows, size), BF16),
            pltpu.VMEM((2 * rows, size), BF16),
            pltpu.VMEM((size, own), F32),
            pltpu.VMEM((2 * rows, own), F32),
            pltpu.VMEM((size, own), F32),
            pltpu.VMEM((size, own), F32),
            pltpu.VMEM((2 * rows, own), F32),
            pltpu.VMEM((2, rows, own), F32),
            dma,
            dma((2,)),
            dma((steps,)),
            dma((3,)),
            dma((2, 4, 2, 2)),
            dma((4, 2, 2)),
            dma((4, steps)),
            dma((4, steps)),
            dma((4, steps)),
            dma((4, steps)),
            dma((10,)),
            dma((10,)),
            dma((10,)),
            dma((10,)),
            dma((3,)),
            dma((5,)),
            dma((2,)),
            dma((2,)),
            dma((2,)),
            dma((2,)),
        ],
        compiler_params=pltpu.CompilerParams(
            collective_id=0, has_side_effects=True, vmem_limit_bytes=61 * 1024 * 1024
        ),
    )(panel, prior_y, right_side, inv_blocks, lower_block)


def general(panel, prior_y, right_side, inv_blocks, lower_block):
    highest = lax.Precision.HIGHEST
    terms = jnp.einsum(
        "sip,pm->sim",
        panel,
        lax.all_gather(prior_y, "row", axis=1, tiled=True),
        precision=highest,
        preferred_element_type=jnp.float32,
    )
    panel_total = lax.psum_scatter(terms, "col", scatter_dimension=2, tiled=True)
    residual = right_side - panel_total
    first_all_rows = lax.all_gather(residual[0], "row", axis=0, tiled=True)
    first_solution = jnp.dot(
        inv_blocks[0], first_all_rows, precision=highest, preferred_element_type=jnp.float32
    )
    solved_all = lax.all_gather(first_solution, "row", axis=0, tiled=True)
    second_residual = residual[1] - jnp.dot(
        lower_block, solved_all, precision=highest, preferred_element_type=jnp.float32
    )
    second_all_rows = lax.all_gather(second_residual, "row", axis=0, tiled=True)
    second_solution = jnp.dot(
        inv_blocks[1], second_all_rows, precision=highest, preferred_element_type=jnp.float32
    )
    return (jnp.stack([first_solution, second_solution]), residual[2:])


def solution(mesh):
    placed = (
        P(None, "row", "col"),
        P("col", "row"),
        P(None, "row", "col"),
        P(None, "row", None),
        P("row", None),
    )
    four_by_eight = mesh.shape["row"] == 4 and mesh.shape["col"] == 8
    return jax.shard_map(
        fused if four_by_eight else general,
        mesh=mesh,
        in_specs=placed,
        out_specs=(P(None, "row", "col"), P(None, "row", "col")),
        check_vma=False,
    )
```

```python
import functools

import jax
import jax.numpy as jnp
from jax import lax
from jax.experimental import pallas as pl
from jax.experimental.pallas import tpu as pltpu
from jax.sharding import PartitionSpec as P

MESH = pl.DeviceIdType.MESH
F32 = jnp.float32
BF16 = jnp.bfloat16


def split(x):
    high = x.astype(BF16)
    return high, (x - high.astype(F32)).astype(BF16)


def kernel(
    panel, prior, right, inv, lower, y_out, pend_out,
    pf, p_hi, p_lo, y_buf, y_cat, core_src, core_dst, part, far_dst, rhs,
    inv0, low2, inv1, inv0_hi, inv0_lo, low2_hi, low2_lo, inv1_hi, inv1_lo,
    r0_all, r1_all, y0_all, s1_all, y1_all, y_land,
    right_sem, own_sem, panel_sem, matrix_sem, y_send, y_recv, core_send, core_recv, far_send, far_recv,
    m_send, m_recv, twin_send, twin_recv, r_send, r_recv, s_send, s_recv, e_send, e_recv,
):
    steps, rows, depth = p_hi.shape
    wide = rhs.shape[2]
    staged = pf.shape[0]
    half, part_rows = depth // 2, rows // 2
    lag = 2
    z = lax.axis_index("row")
    col = lax.axis_index("col")
    y, x, core = col // 4, (col // 2) % 2, col % 2
    chip = col // 2
    sibling = col + 1 - 2 * core
    x_near, y_near = col + 2 - 4 * x, col + 4 - 8 * y
    middle = (z == 1) | (z == 2)
    upper = z // 2
    inner = ((z + 1) // 2) % 2
    line = chip + upper * (3 - 2 * chip)
    z_end, z_other = 3 * upper, 1 + upper + inner * (1 - 2 * upper)

    def block(folded):
        return folded + upper * (3 - 2 * folded)

    def number(digits):
        return sum(d * 8**i for i, d in enumerate(digits))

    line_y, line_x = line // 2, line % 2
    at_end = (1 - line_y) * number((0, 1, 2, 4, 6, 7, 5, 3)) + line_y * (
        (1 - line_x) * number((0, 1, 2, 3, 4, 6, 7, 5)) + line_x * number((0, 1, 2, 3, 4, 6, 5, 7))
    )
    sequence = at_end + inner * (number((2, 3, 0, 4, 1, 6, 7, 5)) - at_end)

    def turn(k):
        digit = (sequence // 8**k) % 8
        return block(digit // 2), digit % 2

    own = [
        pltpu.make_async_copy(prior.at[:, h * wide:(h + 1) * wide], y_buf.at[z, h], own_sem.at[h])
        for h in range(2)
    ]
    for copy in own:
        copy.start()

    def panel_copy(s):
        return pltpu.make_async_copy(panel.at[s], pf.at[s % staged], panel_sem.at[s])

    for s in range(staged):
        panel_copy(s).start()
    right_copy = pltpu.make_async_copy(right, rhs, right_sem)
    right_copy.start()

    barrier = pltpu.get_barrier_semaphore()
    for partner in (sibling, x_near, y_near, x_near + y_near - col):
        pl.semaphore_signal(barrier, inc=1, device_id=(z, partner), device_id_type=MESH)
    for j in range(1, 4):
        pl.semaphore_signal(barrier, inc=1, device_id=((z + j) % 4, col), device_id_type=MESH)
    pl.semaphore_wait(barrier, 7)

    def remote(src, dst, send, recv, target):
        return pltpu.make_async_remote_copy(
            src_ref=src, dst_ref=dst, send_sem=send, recv_sem=recv,
            device_id=target, device_id_type=MESH,
        )

    def y_piece(b, h, p):
        return y_buf.at[b, h, pl.ds(p * half, half)]

    def y_copy(folded, h, p, way, from_prior=False):
        b = block(folded)
        here = y_piece(b, h, p)
        src = prior.at[pl.ds(p * half, half), pl.ds(h * wide, wide)] if from_prior else here
        target = z_other if way else z_end
        return remote(src, here, y_send.at[way, folded, h, p], y_recv.at[b, h, p], (target, col))

    def arrived(b, h, p):
        remote(
            y_piece(b, h, p), y_piece(b, h, p), y_send.at[0, 0, h, p], y_recv.at[b, h, p],
            ((z + 1) % 4, col),
        ).wait_recv()

    def outward(folded, h, p):
        y_copy(folded, h, p, 0, folded == 1).start()

    def inward(folded, h, p):
        y_copy(folded, h, p, 1, folded == 1).start()

    def relay(k):
        def take(folded, h, p):
            arrived(block(folded), h, p)

        if k == 0:
            for p in range(2):
                outward(1, 0, p)
                inward(1, 0, p)

            @pl.when(line > 1)
            def _():
                outward(1, 1, 0)
                outward(1, 1, 1)
        elif k in (1, 2):
            take(0, 0, k - 1)
            inward(0, 0, k - 1)
            take(2, 0, k - 1)
            outward(2, 0, k - 1)
        elif k in (3, 4):
            take(0, 1, k - 3)
            inward(0, 1, k - 3)
            if k == 4:
                inward(1, 1, 0)
                inward(1, 1, 1)
            take(3, 0, k - 3)
            outward(3, 0, k - 3)
        elif k == 5:
            take(3, 1, 0)
            pl.when(line != 3)(lambda: outward(3, 1, 0))
        elif k == 6:
            take(3, 1, 1)
            pl.when(line != 3)(lambda: outward(3, 1, 1))
        else:
            for p in range(2):
                take(2, 1, p)
                outward(2, 1, p)
            for p in range(2):
                pl.when(line == 3)(lambda p=p: outward(3, 1, p))
                pl.when(line < 2)(lambda p=p: outward(1, 1, p))

    def core_copy(b, c):
        return remote(
            core_src.at[b, c], core_dst.at[b, c], core_send.at[b, c], core_recv.at[b, c], (z, sibling)
        )

    def detour(b):
        both = block(b) + line
        return (1 - inner) * (1 - line_y) * (both // 3 - both // 4)

    def passes(b):
        return jnp.logical_not(middle) & (block(b) == line + 2)

    def far_copy(b, c):
        slot = (x + b) % 2 + 2 * ((y + b // 2) % 2) - 1
        target = 2 * b + core
        return remote(
            part.at[b, c], far_dst.at[slot + detour(b) * (3 - slot), c],
            far_send.at[b, c], far_recv.at[slot + detour(b) * (3 - slot), c],
            (z, target + detour(b) * (x_near - target)),
        )

    def far_arrived(slot, c):
        here = far_dst.at[slot, c]
        remote(here, here, far_send.at[0, c], far_recv.at[slot, c], (z, sibling)).wait_recv()

    def add_core(b, c):
        core_copy(b, c).wait_recv()
        part[b, c] = part[b, c] + core_dst[b, c]

        @pl.when((b != chip) & jnp.logical_not(passes(b)))
        def _():
            far_copy(b, c).start()

    def pass_on(b, low, high):
        @pl.loop(low, high)
        def _(c):
            far_arrived(3, c)
            part[b, c] = part[b, c] + far_dst[3, c]
            far_copy(b, c).start()

    def multiply(k, b, h):
        high, low = split(y_buf[b, h])
        y_cat[:, :wide] = high
        y_cat[:, wide:] = low

        @pl.loop(0, steps)
        def _(c):
            if k == 0:
                panel_copy(c).wait()
                high, low = split(pf[c % staged])
                p_hi[c] = high
                p_lo[c] = low

                @pl.when(c < steps - staged)
                def _():
                    panel_copy(c + staged).start()
            both = jnp.dot(p_hi[c], y_cat[...], preferred_element_type=F32)
            rest = jnp.dot(p_lo[c], y_cat[:, :wide], preferred_element_type=F32)
            terms = both[:, :wide] + (both[:, wide:] + rest)

            @pl.when(core == h)
            def _():
                part[b, c] = terms

                @pl.when(c >= lag)
                def _():
                    add_core(b, c - lag)

            @pl.when(core != h)
            def _():
                core_src[b, c] = terms
                core_copy(b, c).start()

        @pl.when(core == h)
        def _():
            for c in range(steps - lag, steps):
                add_core(b, c)

    def multiply_last(b, h, before, wait_last):
        groups = ((0, 2), (2, 4), (4, 6), (6, 8))
        for p in range(2):
            here = slice(p * half, (p + 1) * half)
            if p == 1:
                wait_last()
            high, low = split(y_buf[b, h, here])
            y_cat[here, :wide] = high
            y_cat[here, wide:] = low

            def product(c, count):
                left = p_hi[pl.ds(c, count), :, here].reshape(count * rows, half)
                both = jnp.dot(left, y_cat[here, :], preferred_element_type=F32)
                left = p_lo[pl.ds(c, count), :, here].reshape(count * rows, half)
                rest = jnp.dot(left, y_cat[here, :wide], preferred_element_type=F32)
                return (both[:, :wide] + (both[:, wide:] + rest)).reshape(count, rows, wide)

            if p == 0:
                @pl.loop(0, steps // 2)
                def _(i):
                    terms = product(2 * i, 2)

                    @pl.when(core == h)
                    def _():
                        part[b, pl.ds(2 * i, 2)] = terms

                    @pl.when(core != h)
                    def _():
                        core_src[b, pl.ds(2 * i, 2)] = terms
                continue
            for i, (low_c, high_c) in enumerate(groups):
                terms = product(low_c, high_c - low_c)

                @pl.when(core == h)
                def _():
                    part[b, low_c:high_c] = part[b, low_c:high_c] + terms
                    if i > 0:
                        for c in range(*groups[i - 1]):
                            add_core(b, c)

                @pl.when(core != h)
                def _():
                    core_src[b, low_c:high_c] = core_src[b, low_c:high_c] + terms
                    for c in range(low_c, high_c):
                        core_copy(b, c).start()
                if i == 1:
                    @pl.when(jnp.logical_not(middle) & (core == 1) & (line > 1))
                    def _():
                        finish(0, 2)
                if i == 2:
                    pl.when(before[1])(lambda: pass_on(before[0], 2, 3))
                if i == 3:
                    pl.when(before[1])(lambda: pass_on(before[0], 3, 4))

        @pl.when(core == h)
        def _():
            for c in range(*groups[-1]):
                add_core(b, c)
        pl.when(before[1])(lambda: pass_on(before[0], 4, steps))

    matrices = (
        (0, 1, 0), (0, 1, 1), (0, 1, 2), (0, 2, 0), (1, 2, 0),
        (2, 1, 0), (3, 2, 0), (3, 1, 0), (3, 2, 1), (3, 2, 2),
    )

    def matrix_refs(source, kind, half_of):
        width = (source + 1) * rows
        take = pl.ds(half_of * part_rows, part_rows)
        if kind == 0:
            put = pl.ds(pl.multiple_of(source * rows + half_of * part_rows, part_rows), part_rows)
            return inv.at[0, take, :width], inv0.at[put, :width]
        put = pl.ds(pl.multiple_of((source % 2) * rows + half_of * part_rows, part_rows), part_rows)
        if kind == 1:
            return lower.at[take], low2.at[put]
        return inv.at[1, take, :width], inv1.at[put, :width]

    def matrix_copy(i):
        source, target, kind = matrices[i]
        src, dst = matrix_refs(source, kind, core)
        return remote(src, dst, m_send.at[i], m_recv.at[i], (target, col))

    def twin_copy(i):
        source, _, kind = matrices[i]
        here = matrix_refs(source, kind, core)[1]
        return remote(here, here, twin_send.at[i], twin_recv.at[i], (z, sibling))

    def send_matrices(which, finish=False):
        for i, (source, _, _) in enumerate(matrices):
            if i in which:
                @pl.when(z == source)
                def _(i=i):
                    matrix_copy(i).wait_send() if finish else matrix_copy(i).start()

    place = pl.ds(pl.multiple_of((z % 2) * rows, rows), rows)
    mine = pl.ds(pl.multiple_of(z * rows, rows), rows)
    own_matrices = [
        pltpu.make_async_copy(inv.at[0], inv0.at[mine], matrix_sem.at[0]),
        pltpu.make_async_copy(lower, low2.at[place], matrix_sem.at[1]),
        pltpu.make_async_copy(inv.at[1], inv1.at[place], matrix_sem.at[2]),
    ]

    def r0_copy(target, source):
        here = r0_all.at[pl.ds(pl.multiple_of(source * rows, rows), rows)]
        return remote(here, here, r_send.at[target], r_recv.at[source], (target, col))

    def r1_copy():
        here = r1_all.at[place]
        return remote(here, here, r_send.at[0], r_recv.at[4], (z_other, col))

    def r1_arrived():
        other = r1_all.at[pl.ds(pl.multiple_of((1 - z % 2) * rows, rows), rows)]
        remote(other, other, r_send.at[0], r_recv.at[4], (z_end, col)).wait_recv()

    def send_r0(finish=False):
        for target in (2, 1):
            @pl.when(z != target)
            def _(target=target):
                r0_copy(target, z).wait_send() if finish else r0_copy(target, z).start()

    def finish(low, high):
        for s in range(low, high):
            for slot in range(2):
                far_arrived(slot, s)
            pl.when(middle | (line < 2))(lambda s=s: far_arrived(2, s))
            total = (part[chip, s] + far_dst[0, s]) + (far_dst[1, s] + far_dst[2, s])
            rest = rhs[s] - total
            if s == 0:
                r0_all[mine, :] = rest
                send_r0()
            elif s == 1:
                r1_all[place, :] = rest
                pl.when(jnp.logical_not(middle))(lambda: r1_copy().start())
            else:
                pend_out[s - 2] = rest

    @pl.when(jnp.logical_not(middle) & (line > 1))
    def _():
        far_dst[2] = jnp.zeros((steps, rows, wide), F32)

    @pl.when(middle)
    def _():
        relay(0)

    @pl.when(jnp.logical_not(middle))
    def _():
        for h in range(2):
            for p in range(2):
                y_copy(0, h, p, 1, True).start()

    for k in range(8):
        b, h = turn(k)
        if k == 7:
            right_copy.wait()

            @pl.when(jnp.logical_not(middle) & ((core == 0) | (line == 0)))
            def _():
                finish(0, steps)

        if k > 0:
            @pl.when(middle)
            def _(k=k):
                relay(k)
        if k < 2:
            own[k].wait()
        else:
            @pl.when(jnp.logical_not(middle))
            def _(b=b, h=h, k=k):
                arrived(b, h, 0)
                if k < 7:
                    arrived(b, h, 1)
        if k == 7:
            multiply_last(b, h, before, lambda: pl.when(jnp.logical_not(middle))(lambda: arrived(b, h, 1)))
            continue
        multiply(k, b, h)
        passing = passes(b) & (core == h)
        if k > 0:
            pl.when(before[1])(lambda: pass_on(before[0], steps // 2, steps))
        early = 2 if k == 6 else steps // 2
        pl.when(passing)(lambda: pass_on(b, 0, early))
        before = b, passing
        if k == 2:
            send_matrices((0, 1, 2, 6, 8, 9))

            @pl.when(middle)
            def _():
                for copy in own_matrices:
                    copy.start()
        if k == 5:
            send_matrices((3, 7))
        if k == 6:
            send_matrices((4, 5))

    def split_rows(ref, hi, lo, first, width):
        high, low = split(ref[first:first + rows, :width])
        hi[first:first + rows, :width] = high
        lo[first:first + rows, :width] = low

    @pl.when(middle)
    def _():
        for copy in own_matrices:
            copy.wait()
        for target in (1, 2):
            @pl.when(z == target)
            def _(target=target):
                here = [i for i, entry in enumerate(matrices) if entry[1] == target]
                for i in here:
                    matrix_copy(i).wait_recv()
                    twin_copy(i).start()
                for i in here:
                    source, _, kind = matrices[i]
                    other = matrix_refs(source, kind, 1 - core)[1]
                    remote(other, other, twin_send.at[i], twin_recv.at[i], (z, sibling)).wait_recv()
                for k in range(2):
                    split_rows(inv1, inv1_hi, inv1_lo, k * rows, (2 * target - 1 + k) * rows)
        for k in range(4):
            split_rows(inv0, inv0_hi, inv0_lo, k * rows, (k + 1) * rows)
        for k in range(2):
            split_rows(low2, low2_hi, low2_lo, k * rows, 4 * rows)

    @pl.when(middle | ((core == 1) & (line == 1)))
    def _():
        finish(0, 2)

    @pl.when(jnp.logical_not(middle) & (core == 1) & (line > 0))
    def _():
        finish(2, steps)

    def dot3(hi, lo, at, width, value, first=0):
        high, low = value
        both = jnp.dot(hi[at, first:width], jnp.concatenate([high, low], axis=1), preferred_element_type=F32)
        rest = jnp.dot(lo[at, first:width], high, preferred_element_type=F32)
        return both[:, :wide] + (both[:, wide:] + rest)

    def end_copy(i, src):
        return remote(src, y_land.at[i], e_send.at[i], e_recv.at[i], (z_end, col))

    def y_ends():
        at_end = pl.ds(pl.multiple_of(z_end * rows, rows), rows)
        far_place = pl.ds(pl.multiple_of((1 - z % 2) * rows, rows), rows)
        return end_copy(0, y0_all.at[at_end]), end_copy(1, y1_all.at[far_place])

    def s_copy(k):
        here = s1_all.at[k * rows:(k + 1) * rows]
        return remote(here, here, s_send.at[k], s_recv.at[k], (2, col))

    @pl.when(middle)
    def _():
        to_end = y_ends()

        def r0_split(source):
            @pl.when(z != source)
            def _():
                r0_copy(1, source).wait_recv()
            return split(r0_all[source * rows:(source + 1) * rows, :])

        def columns(ref_hi, ref_lo, first, source, value):
            high, low = value
            here = slice(source * rows, (source + 1) * rows)
            both = jnp.dot(ref_hi[first:, here], jnp.concatenate([high, low], axis=1), preferred_element_type=F32)
            rest = jnp.dot(ref_lo[first:, here], high, preferred_element_type=F32)
            return both[:, :wide] + (both[:, wide:] + rest)

        for source in (1, 2, 0, 3):
            first = source * rows
            terms = columns(inv0_hi, inv0_lo, first, source, r0_split(source))
            if source == 1:
                y0_all[:rows, :] = jnp.zeros((rows, wide), F32)
                y0_all[rows:, :] = terms
            else:
                y0_all[first:, :] = y0_all[first:, :] + terms
        to_end[0].start()
        r1_arrived()
        solved = split(y0_all[...])

        def second(k):
            at = slice(k * rows, (k + 1) * rows)
            return r1_all[at, :] - dot3(low2_hi, low2_lo, at, 4 * rows, solved)

        def s1_rows(k):
            return s1_all[:k * rows, :]

        @pl.when(z == 1)
        def _():
            for k in range(2):
                s1_all[k * rows:(k + 1) * rows, :] = second(k)
                s_copy(k).start()
            for k in range(2):
                at = slice(k * rows, (k + 1) * rows)
                y1_all[at, :] = dot3(inv1_hi, inv1_lo, at, (k + 1) * rows, split(s1_rows(k + 1)))
                if k == 0:
                    to_end[1].start()

        @pl.when(z == 2)
        def _():
            for k in range(2):
                s1_all[(2 + k) * rows:(3 + k) * rows, :] = second(k)
            own_s1 = split(s1_all[2 * rows:, :])
            for k in range(2):
                at = slice(k * rows, (k + 1) * rows)
                value = tuple(v[:(k + 1) * rows] for v in own_s1)
                y1_all[at, :] = dot3(inv1_hi, inv1_lo, at, (3 + k) * rows, value, 2 * rows)
            for k in range(2):
                s_copy(k).wait_recv()
            far_s1 = split(s1_rows(2))
            for k in (1, 0):
                at = slice(k * rows, (k + 1) * rows)
                y1_all[at, :] = y1_all[at, :] + dot3(inv1_hi, inv1_lo, at, 2 * rows, far_s1)
                if k == 1:
                    to_end[1].start()

        finish(2, steps)
        y_out[0] = y0_all[mine, :]
        y_out[1] = y1_all[place, :]
        for copy in to_end:
            copy.wait_send()

        @pl.when(z == 1)
        def _():
            for k in range(2):
                s_copy(k).wait_send()

        for target in (1, 2):
            @pl.when(z == target)
            def _(target=target):
                for i, entry in enumerate(matrices):
                    if entry[1] == target:
                        twin_copy(i).wait_send()

    @pl.when(jnp.logical_not(middle))
    def _():
        for i in range(2):
            remote(y_land.at[i], y_land.at[i], e_send.at[i], e_recv.at[i], (z_other, col)).wait_recv()
            y_out[i] = y_land[i]
        r1_copy().wait_send()

    send_r0(True)
    send_matrices(range(len(matrices)), True)

    @pl.when(middle)
    def _():
        for h in range(2):
            for p in range(2):
                for folded in (1, 2, 3):
                    y_copy(folded, h, p, 0, folded == 1).wait_send()
                for folded in (0, 1):
                    y_copy(folded, h, p, 1, folded == 1).wait_send()

    @pl.when(jnp.logical_not(middle))
    def _():
        for h in range(2):
            for p in range(2):
                y_copy(0, h, p, 1, True).wait_send()

    for b in range(4):
        @pl.loop(0, steps)
        def _(c):
            core_copy(b, c).wait_send()

            @pl.when(b != chip)
            def _():
                far_copy(b, c).wait_send()


def fused(panel, prior_y, right_side, inv_blocks, lower_block):
    steps, rows, depth = panel.shape
    own = right_side.shape[2]
    size = inv_blocks.shape[2]
    anywhere = pl.BlockSpec(memory_space=pl.ANY)
    local = pl.BlockSpec(memory_space=pltpu.VMEM)
    dma = pltpu.SemaphoreType.DMA
    return pl.pallas_call(
        kernel,
        out_shape=(
            pltpu.VMEM((2, rows, own), F32),
            pltpu.VMEM((steps - 2, rows, own), F32),
        ),
        in_specs=[anywhere] * 5,
        out_specs=(local, local),
        scratch_shapes=[
            pltpu.VMEM((4, rows, depth), F32),
            pltpu.VMEM((steps, rows, depth), BF16),
            pltpu.VMEM((steps, rows, depth), BF16),
            pltpu.VMEM((4, 2, depth, own), F32),
            pltpu.VMEM((depth, 2 * own), BF16),
            pltpu.VMEM((4, steps, rows, own), F32),
            pltpu.VMEM((4, steps, rows, own), F32),
            pltpu.VMEM((4, steps, rows, own), F32),
            pltpu.VMEM((4, steps, rows, own), F32),
            pltpu.VMEM((steps, rows, own), F32),
            pltpu.VMEM((size, size), F32),
            pltpu.VMEM((2 * rows, size), F32),
            pltpu.VMEM((2 * rows, size), F32),
            pltpu.VMEM((size, size), BF16),
            pltpu.VMEM((size, size), BF16),
            pltpu.VMEM((2 * rows, size), BF16),
            pltpu.VMEM((2 * rows, size), BF16),
            pltpu.VMEM((2 * rows, size), BF16),
            pltpu.VMEM((2 * rows, size), BF16),
            pltpu.VMEM((size, own), F32),
            pltpu.VMEM((2 * rows, own), F32),
            pltpu.VMEM((size, own), F32),
            pltpu.VMEM((size, own), F32),
            pltpu.VMEM((2 * rows, own), F32),
            pltpu.VMEM((2, rows, own), F32),
            dma,
            dma((2,)),
            dma((steps,)),
            dma((3,)),
            dma((2, 4, 2, 2)),
            dma((4, 2, 2)),
            dma((4, steps)),
            dma((4, steps)),
            dma((4, steps)),
            dma((4, steps)),
            dma((10,)),
            dma((10,)),
            dma((10,)),
            dma((10,)),
            dma((3,)),
            dma((5,)),
            dma((2,)),
            dma((2,)),
            dma((2,)),
            dma((2,)),
        ],
        compiler_params=pltpu.CompilerParams(
            collective_id=0, has_side_effects=True, vmem_limit_bytes=61 * 1024 * 1024
        ),
    )(panel, prior_y, right_side, inv_blocks, lower_block)


def general(panel, prior_y, right_side, inv_blocks, lower_block):
    highest = lax.Precision.HIGHEST
    terms = jnp.einsum(
        "sip,pm->sim",
        panel,
        lax.all_gather(prior_y, "row", axis=1, tiled=True),
        precision=highest,
        preferred_element_type=jnp.float32,
    )
    panel_total = lax.psum_scatter(terms, "col", scatter_dimension=2, tiled=True)
    residual = right_side - panel_total
    first_all_rows = lax.all_gather(residual[0], "row", axis=0, tiled=True)
    first_solution = jnp.dot(
        inv_blocks[0], first_all_rows, precision=highest, preferred_element_type=jnp.float32
    )
    solved_all = lax.all_gather(first_solution, "row", axis=0, tiled=True)
    second_residual = residual[1] - jnp.dot(
        lower_block, solved_all, precision=highest, preferred_element_type=jnp.float32
    )
    second_all_rows = lax.all_gather(second_residual, "row", axis=0, tiled=True)
    second_solution = jnp.dot(
        inv_blocks[1], second_all_rows, precision=highest, preferred_element_type=jnp.float32
    )
    return (jnp.stack([first_solution, second_solution]), residual[2:])


def solution(mesh):
    placed = (
        P(None, "row", "col"),
        P("col", "row"),
        P(None, "row", "col"),
        P(None, "row", None),
        P("row", None),
    )
    four_by_eight = mesh.shape["row"] == 4 and mesh.shape["col"] == 8
    return jax.shard_map(
        fused if four_by_eight else general,
        mesh=mesh,
        in_specs=placed,
        out_specs=(P(None, "row", "col"), P(None, "row", "col")),
        check_vma=False,
    )
```
